32 devices in a mesh: ctx: 4 (over z), tp: 4 (over y, x), dp: 2 (over core).
Axes of the slice: x: 2, y: 2, z: 4, core: 2. Of those that a mesh axis runs over, the one named last changes fastest.
Arguments:
- queries: bfloat16 [6144, 2048], P(('dp', 'ctx'), 'tp'), parts along dimension 0, may hold values from -6 to 6
- key_rows: bfloat16 [6144, 2048], P(('dp', 'ctx'), 'tp'), parts along dimension 0, may hold values from -6 to 6
- values: bfloat16 [6144, 2048], P(('dp', 'ctx'), 'tp'), parts along dimension 0, may hold values from -6 to 6
- doc_lengths: int32 [16], P('dp'), parts along dimension 0, may hold values from 1 to 2304, 3072 in all
- in_gate: bfloat16 [6144, 2048], P(('dp', 'ctx'), 'tp'), parts along dimension 0, may hold values from -6 to 6
- out_gate: bfloat16 [6144, 2048], P(('dp', 'ctx'), 'tp'), parts along dimension 0, may hold values from -6 to 6
- filter_taps: float32 [4096, 3072], P(('dp', 'tp'), 'ctx'), parts along dimension 0, may hold values from -0.21875 to 0.21875
Outputs:
- attn_out: bfloat16 [6144, 2048], P(('dp', 'ctx'), 'tp'), parts along dimension 0
- hyena_out: bfloat16 [6144, 2048], P(('dp', 'ctx'), 'tp'), parts along dimension 0
The draws below stay inside these ranges and needn't reach their ends.
There are 2 independent parts, one for each index of `dp`. The reference program is written for one: setup_inputs(seed, part) draws one part's arguments, and reference() takes and returns one part's arrays. A program takes and returns all parts, laid end to end along the dimension named above; each array names one. Nothing has to cross between parts.
Inputs may be any that keep to these rules, and one draw needn't show every extreme that they name: `doc_lengths`: the lengths sum to 3072, and the longest is exactly 2304.
All inputs are finite; a program needn't handle non-finite values.
Results may differ from the reference program's by a relative error of at most 0.012.
Values may be sent and summed in bfloat16 or wider, within the bound.
A program may use at most 192 MiB of HBM per device.

```python
import math
import jax
import jax.numpy as jnp
import numpy as np
from jax import lax

HEADS = 16
HEAD_DIM = 128
TOK_DEV = 768
KV_REACH = 3
CHANNELS = 2048
SEQ = 3072
DOCS = 8
MOST_DOC = 2304


def paired_rows(key):
    folded = jax.random.fold_in(key, 4217)
    query_seed, key_seed = jax.random.split(folded, 2)
    channels = HEADS * HEAD_DIM
    query_draw = jnp.clip(jax.random.normal(query_seed, (SEQ, channels), jnp.float32), -6.0, 6.0)
    key_draw = jnp.clip(jax.random.normal(key_seed, (SEQ, channels), jnp.float32), -6.0, 6.0)
    return (query_draw, key_draw)


def draw_queries(key, part):
    return paired_rows(key)[0].astype(jnp.bfloat16)


def draw_key_rows(key, part):
    return paired_rows(key)[1].astype(jnp.bfloat16)


def levels(rng, shape, cuts, smallest, high):
    factor_of = 1.0
    for position, blocks in cuts:
        heights = jax.random.uniform(jax.random.fold_in(jax.random.fold_in(rng, 6), position), (blocks,), jnp.float32, smallest / len(cuts), high / len(cuts))
        factor_of = factor_of * jnp.repeat(jnp.exp(heights), shape[position] // blocks).reshape((-1,) + (1,) * (len(shape) - 1 - position))
    return factor_of


def split_up(amount, total, bound, slope):
    portions = [(1 << 20) // math.isqrt(grade ** slope) + 1 for grade in range(2, amount + 1)]
    spare, given = total - bound - (amount - 1), [1] * (amount - 1)
    while spare > 0:
        candidates = [i for i in range(amount - 1) if given[i] < bound]
        whole, budget = sum([portions[i] for i in candidates]), spare
        for i in candidates:
            extra = min(bound - given[i], max(1, budget * portions[i] // whole), spare)
            given[i] = given[i] + extra
            spare = spare - extra
    return np.array([bound] + given)


def ragged(key, number_of, total, most, slope):
    if number_of == 2:
        one = jax.random.randint(key, (), max(1, total - most), min(most, total - 1) + 1)
        return jnp.stack([one, total - one])
    tallies = jnp.asarray(split_up(number_of, total, most, slope), jnp.int32)
    twos = (number_of - 1) // 2
    giver, taker = tallies[1:1 + 2 * twos:2], tallies[2:2 + 2 * twos:2]
    room = jnp.minimum(giver - 1, most - taker)
    shifted = jax.random.randint(jax.random.fold_in(key, 1), (twos,), 0, 1 << 20) % (room + 1)
    tallies = tallies.at[1:1 + 2 * twos:2].set(giver - shifted).at[2:2 + 2 * twos:2].set(taker + shifted)
    return tallies[jax.random.permutation(jax.random.fold_in(key, 2), number_of)]


def noise(stream_key, extent, scale, most, cuts=(), held_as=jnp.bfloat16):
    factor_of = levels(stream_key, extent, cuts, -0.22, 0.18) if cuts else 1.0
    entries = jax.random.normal(stream_key, extent, jnp.float32) * scale * factor_of
    return jnp.minimum(jnp.maximum(entries, -most), most).astype(held_as)


def setup_inputs(seed: int = 0, part: int = 0) -> dict:
    key_list = jax.random.split(jax.random.key(seed), 8)
    part_keys = jax.random.split(jax.random.fold_in(key_list[7], part), 8)
    return {
        "queries": draw_queries(jax.random.fold_in(jax.random.fold_in(key_list[7], part), 71), part),
        "key_rows": draw_key_rows(jax.random.fold_in(jax.random.fold_in(key_list[7], part), 71), part),
        "values": noise(part_keys[2], (SEQ, CHANNELS), 1.0, 6.0, ((0, 4), (1, 4))),
        "doc_lengths": ragged(part_keys[3], DOCS, SEQ, MOST_DOC, 2).astype(jnp.int32),
        "in_gate": noise(part_keys[4], (SEQ, CHANNELS), 1.0, 6.0, ((0, 4), (1, 4))),
        "out_gate": noise(part_keys[5], (SEQ, CHANNELS), 1.0, 6.0, ((0, 4), (1, 4))),
        "filter_taps": noise(part_keys[6], (CHANNELS, SEQ), (SEQ // 4) ** -0.5, 0.21875, ((0, 4), (1, 4)), jnp.float32),
    }


masked_score = -1e+30

def doc_of(positions, doc_lengths):
    starts = jnp.cumsum(doc_lengths) - doc_lengths
    inside = (starts[None, :] <= positions[:, None]).astype(jnp.int32)
    return lax.optimization_barrier(jnp.sum(inside, axis=1)) - 1

def reference(queries, key_rows, values, doc_lengths, in_gate, out_gate, filter_taps):
    channels = queries.shape[1]
    head_count = channels // HEAD_DIM
    positions = jnp.arange(SEQ, dtype=jnp.int32)
    doc_index = doc_of(positions, doc_lengths)
    reach = KV_REACH * TOK_DEV
    window = reach + TOK_DEV
    padded_keys = jnp.concatenate([jnp.zeros((reach, channels), jnp.bfloat16), key_rows], axis=0)
    padded_values = jnp.concatenate([jnp.zeros((reach, channels), jnp.bfloat16), values], axis=0)
    padded_docs = jnp.concatenate([jnp.full((reach,), -1, jnp.int32), doc_index])
    padded_pos = jnp.concatenate([jnp.arange(reach, dtype=jnp.int32) - reach, positions])

    def one_block(block_index):
        block_start = (block_index * TOK_DEV).astype(jnp.int32)
        query_block = lax.dynamic_slice_in_dim(queries, block_start, TOK_DEV, 0).astype(jnp.float32).reshape(TOK_DEV, head_count, HEAD_DIM)
        query_pos = lax.dynamic_slice_in_dim(positions, block_start, TOK_DEV, 0)
        query_doc = lax.dynamic_slice_in_dim(doc_index, block_start, TOK_DEV, 0)
        key_block = lax.dynamic_slice_in_dim(padded_keys, block_start, window, 0).astype(jnp.float32).reshape(window, head_count, HEAD_DIM)
        value_block = lax.dynamic_slice_in_dim(padded_values, block_start, window, 0).astype(jnp.float32).reshape(window, head_count, HEAD_DIM)
        key_doc = lax.dynamic_slice_in_dim(padded_docs, block_start, window, 0)
        key_pos = lax.dynamic_slice_in_dim(padded_pos, block_start, window, 0)
        allowed = (key_doc[None, :] == query_doc[:, None]) & (key_pos[None, :] <= query_pos[:, None])
        scores = jnp.einsum('qhd,khd->hqk', query_block, key_block) / math.sqrt(HEAD_DIM)
        scores = jnp.where(allowed[None], scores, masked_score)
        top_score = lax.optimization_barrier(jnp.max(scores, axis=2, keepdims=True))
        exp_scores = jnp.exp(scores - top_score)
        row_total = lax.optimization_barrier(jnp.sum(exp_scores, axis=2))
        rounded = lax.optimization_barrier(exp_scores.astype(jnp.bfloat16)).astype(jnp.float32)
        attended = jnp.einsum('hqk,khd->qhd', rounded, value_block) / row_total.T[:, :, None]
        return attended.reshape(TOK_DEV, channels).astype(jnp.bfloat16)
    blocks = lax.map(one_block, jnp.arange(SEQ // TOK_DEV, dtype=jnp.int32))
    attn_out = blocks.reshape(SEQ, channels)
    gated = in_gate.astype(jnp.float32) * attn_out.astype(jnp.float32)
    length = 2 * SEQ
    spectrum = jnp.fft.rfft(gated, n=length, axis=0) * jnp.fft.rfft(filter_taps.T, n=length, axis=0)
    mixed = jnp.fft.irfft(spectrum, n=length, axis=0)[:SEQ]
    hyena_out = (out_gate.astype(jnp.float32) * mixed).astype(jnp.bfloat16)
    return (attn_out, hyena_out)
```

```python
import math

import jax
import jax.numpy as jnp
import numpy as np
from jax import lax
from jax.experimental import pallas as pl
from jax.experimental.pallas import tpu as pltpu
from jax.sharding import PartitionSpec as P

HEAD_DIM = 128
KV_REACH = 3
BLOCK = 256


masked_score = -1e30


def passed_along(x, axis, by):
    length = lax.axis_size(axis)
    pairs = [(i, i + by) for i in range(length) if 0 <= i + by < length]
    return lax.ppermute(x, axis, pairs)


def doc_of(positions, doc_lengths):
    starts = jnp.cumsum(doc_lengths) - doc_lengths
    inside = (starts[None, :] <= positions[:, None]).astype(jnp.int32)
    return jnp.sum(inside, axis=1) - 1


def attend_block(carried, pair, query_heads, allowed):
    running_max, running_sum, weighted = carried
    row_count = query_heads.shape[0]
    key_heads = pair[0].reshape(row_count, -1, HEAD_DIM)
    value_heads = pair[1].reshape(row_count, -1, HEAD_DIM)
    scores = jnp.einsum(
        "qhd,khd->hqk", query_heads, key_heads, preferred_element_type=jnp.float32
    ) / math.sqrt(HEAD_DIM)
    scores = jnp.where(allowed[None], scores, masked_score)
    new_max = jnp.maximum(running_max, jnp.max(scores, axis=2))
    rescale = jnp.exp(running_max - new_max)
    exp_scores = jnp.exp(scores - new_max[:, :, None])
    running_sum = running_sum * rescale + jnp.sum(exp_scores, axis=2)
    weighted = weighted * rescale[:, :, None] + jnp.einsum(
        "hqk,khd->hqd",
        exp_scores.astype(jnp.bfloat16),
        value_heads,
        preferred_element_type=jnp.float32,
    )
    return (new_max, running_sum, weighted)


def split_parts(source):
    high_part = lax.optimization_barrier(source.astype(jnp.bfloat16))
    low_part = (source - high_part.astype(jnp.float32)).astype(jnp.bfloat16)
    return (high_part, low_part)


def split_mul(form, left_parts, right_parts):
    first = jnp.einsum(form, left_parts[0], right_parts[0], preferred_element_type=jnp.float32)
    second = jnp.einsum(form, left_parts[0], right_parts[1], preferred_element_type=jnp.float32)
    third = jnp.einsum(form, left_parts[1], right_parts[0], preferred_element_type=jnp.float32)
    return first + (second + third)


def dft_tables(length):
    inner_len = math.gcd(length, 256)
    outer_len = 2 * length // inner_len
    freq_rows = jnp.arange(outer_len, dtype=jnp.int32)
    time_rows = jnp.arange(outer_len // 2, dtype=jnp.int32)
    inner_index = jnp.arange(inner_len, dtype=jnp.int32)
    angle_outer = (
        2.0
        * math.pi
        / outer_len
        * (freq_rows[:, None] * time_rows[None, :] % outer_len).astype(jnp.float32)
    )
    angle_twist = (
        2.0
        * math.pi
        / (2 * length)
        * (freq_rows[:, None] * inner_index[None, :] % (2 * length)).astype(jnp.float32)
    )
    angle_inner = (
        2.0
        * math.pi
        / inner_len
        * (inner_index[:, None] * inner_index[None, :] % inner_len).astype(jnp.float32)
    )
    return (
        split_parts(jnp.cos(angle_outer)),
        split_parts(-jnp.sin(angle_outer)),
        jnp.cos(angle_twist),
        -jnp.sin(angle_twist),
        split_parts(jnp.cos(angle_inner)),
        split_parts(-jnp.sin(angle_inner)),
    )


def right_mul(left_parts, table_parts):
    return split_mul("cin,nm->cim", left_parts, table_parts)


def forward_dft(samples, tables):
    outer_cos, outer_sin, twist_cos, twist_sin, inner_cos, inner_sin = tables
    item_count = samples.shape[0]
    shaped = split_parts(samples.reshape(item_count, outer_cos[0].shape[1], inner_cos[0].shape[0]))
    section_real = split_mul("ij,cjn->cin", outer_cos, shaped)
    section_imag = split_mul("ij,cjn->cin", outer_sin, shaped)
    turned_real = split_parts(section_real * twist_cos - section_imag * twist_sin)
    turned_imag = split_parts(section_real * twist_sin + section_imag * twist_cos)
    spec_real = right_mul(turned_real, inner_cos) - right_mul(turned_imag, inner_sin)
    spec_imag = right_mul(turned_real, inner_sin) + right_mul(turned_imag, inner_cos)
    return (spec_real, spec_imag)


def inverse_dft(prod_real, prod_imag, tables):
    outer_cos, outer_sin, twist_cos, twist_sin, inner_cos, inner_sin = tables
    item_count = prod_real.shape[0]
    half_len = outer_cos[0].shape[1]
    inner_len = inner_cos[0].shape[0]
    real_parts = split_parts(prod_real)
    imag_parts = split_parts(prod_imag)
    back_real = right_mul(real_parts, inner_cos) + right_mul(imag_parts, inner_sin)
    back_imag = right_mul(imag_parts, inner_cos) - right_mul(real_parts, inner_sin)
    unturn_real = split_parts(back_real * twist_cos + back_imag * twist_sin)
    unturn_imag = split_parts(back_imag * twist_cos - back_real * twist_sin)
    rows_out = split_mul("ij,cin->cjn", outer_cos, unturn_real) + split_mul(
        "ij,cin->cjn", outer_sin, unturn_imag
    )
    return (rows_out * (1.0 / (2 * half_len * inner_len))).reshape(item_count, half_len * inner_len)


def filter_apply(signal, filter_spec, tables):
    sig_real, sig_imag = forward_dft(signal, tables)
    tap_real, tap_imag = filter_spec
    prod_real = sig_real * tap_real - sig_imag * tap_imag
    prod_imag = sig_real * tap_imag + sig_imag * tap_real
    return inverse_dft(prod_real, prod_imag, tables)


def body(queries, key_rows, values, doc_lengths, in_gate, out_gate, filter_taps):
    row_count, channels = queries.shape
    head_count = channels // HEAD_DIM
    group_count = lax.axis_size("ctx")
    per_group = channels // group_count
    seq_len = row_count * group_count
    tables = dft_tables(seq_len)
    taps_grouped = filter_taps.reshape(group_count, per_group, row_count)
    query_pos = lax.axis_index("ctx") * row_count + jnp.arange(row_count, dtype=jnp.int32)
    query_doc = doc_of(query_pos, doc_lengths)
    query_heads = queries.reshape(row_count, head_count, HEAD_DIM)
    carried = (
        jnp.full((head_count, row_count), masked_score, jnp.float32),
        jnp.zeros((head_count, row_count), jnp.float32),
        jnp.zeros((head_count, row_count, HEAD_DIM), jnp.float32),
    )

    def visit(state_now, pair, distance):
        key_pos = query_pos - distance * row_count
        key_doc = doc_of(key_pos, doc_lengths)
        allowed = (key_doc[None, :] == query_doc[:, None]) & (
            key_pos[None, :] <= query_pos[:, None]
        )
        return lax.cond(
            jnp.any(allowed),
            lambda state_in: attend_block(state_in, pair, query_heads, allowed),
            lambda state_in: state_in,
            state_now,
        )

    own_pair = jnp.stack((key_rows, values))
    carried = visit(carried, own_pair, 0)
    moving = own_pair
    for distance in range(1, KV_REACH + 1):
        moving = passed_along(moving, "ctx", 1)
        carried = visit(carried, moving, distance)
    running_max, running_sum, weighted = carried
    attended = (
        (weighted / running_sum[:, :, None])
        .transpose(1, 0, 2)
        .reshape(row_count, channels)
        .astype(jnp.bfloat16)
    )
    gated = (in_gate.astype(jnp.float32) * attended.astype(jnp.float32)).T
    gated_grouped = gated.reshape(group_count, per_group, row_count)
    pair = (
        lax.all_to_all(
            gated_grouped.astype(jnp.bfloat16), "ctx", split_axis=0, concat_axis=2, tiled=True
        ).astype(gated_grouped.dtype),
        lax.all_to_all(
            taps_grouped.astype(jnp.bfloat16), "ctx", split_axis=0, concat_axis=2, tiled=True
        ).astype(taps_grouped.dtype),
    )
    item_count = pair[0].shape[1]
    signal = pair[0].reshape(item_count, -1)
    taps = pair[1].reshape(item_count, -1)
    result = filter_apply(signal, forward_dft(taps, tables), tables)
    mixed = result.reshape(1, item_count, -1)
    returned = lax.all_to_all(
        mixed.astype(jnp.bfloat16), "ctx", split_axis=2, concat_axis=0, tiled=True
    ).astype(mixed.dtype)
    hyena_out = (out_gate.astype(jnp.float32) * returned.reshape(channels, row_count).T).astype(
        jnp.bfloat16
    )
    return (attended, hyena_out)


def block_tables(block):
    freq = np.arange(block)
    time = np.arange(block)
    angle = np.pi / (2 * block) * ((2 * freq[:, None] + 1) * time[None, :] % (4 * block))
    forward = np.concatenate((np.cos(angle), -np.sin(angle)), axis=0)
    inverse = forward.T / block
    return (jnp.asarray(forward, jnp.bfloat16), jnp.asarray(inverse, jnp.bfloat16))


def fused_kernel(
    docs_ref,
    query_ref,
    key_ref,
    value_ref,
    gate_ref,
    taps_ref,
    out_gate_ref,
    forward_ref,
    inverse_ref,
    attn_ref,
    hyena_ref,
    all_query,
    all_key,
    all_value,
    all_gate,
    all_taps,
    own_out_gate,
    score_buf,
    attn_buf,
    sig_spec,
    tap_spec,
    prod_spec,
    mixed_buf,
    mixed_back,
    send_sem,
    recv_sem,
    local_sem,
):
    rows, _ = query_ref.shape
    length, width = all_query.shape
    groups = length // rows
    block = inverse_ref.shape[0]
    blocks = length // block
    per_row = rows // block
    reach = KV_REACH * per_row
    me = lax.axis_index("ctx")

    def rows_of(group):
        return pl.ds(pl.multiple_of(group * rows, rows), rows)

    def cols_of(group):
        return pl.ds(pl.multiple_of(group * width, width), width)

    barrier = pltpu.get_barrier_semaphore()
    for step in range(1, groups):
        peer = lax.rem(me + step, groups)
        pl.semaphore_signal(
            barrier, inc=1, device_id={"ctx": peer}, device_id_type=pl.DeviceIdType.MESH
        )
    pl.semaphore_wait(barrier, groups - 1)

    def remote(source, target, kind, step):
        return pltpu.make_async_remote_copy(
            src_ref=source,
            dst_ref=target,
            send_sem=send_sem.at[kind, step],
            recv_sem=recv_sem.at[kind, step],
            device_id={"ctx": lax.rem(me + step, groups)},
            device_id_type=pl.DeviceIdType.MESH,
        )

    def inbound(kind, step):
        peer = lax.rem(me + step, groups)
        source_of = (query_ref, key_ref, value_ref, gate_ref)
        target_of = (all_query, all_key, all_value, all_gate)
        if kind == 4:
            return (
                taps_ref.at[rows_of_width(peer), :],
                all_taps.at[:, rows_of(me)],
            )
        return (source_of[kind].at[:, cols_of(peer)], target_of[kind].at[rows_of(me), :])

    def rows_of_width(group):
        return pl.ds(pl.multiple_of(group * width, width), width)

    sends = {}
    own = {}
    for kind in range(5):
        for step in range(1, groups):
            source, target = inbound(kind, step)
            sends[kind, step] = remote(source, target, kind, step)
            sends[kind, step].start()
    for kind in range(5):
        source, target = inbound(kind, 0)
        own[kind] = pltpu.make_async_copy(source, target, local_sem.at[kind])
        own[kind].start()
    gate_copy = pltpu.make_async_copy(out_gate_ref, own_out_gate, local_sem.at[5])
    gate_copy.start()

    def arrive(kind):
        own[kind].wait()
        for step in range(1, groups):
            sends[kind, step].wait_recv()

    starts = []
    total = jnp.int32(0)
    for doc in range(docs_ref.shape[0]):
        starts.append(total)
        total = total + docs_ref[doc]

    for kind in range(3):
        arrive(kind)

    def query_tile(tile):
        low = jnp.maximum(tile - reach, 0)
        row0 = pl.multiple_of(tile * block, block)
        query = all_query[pl.ds(row0, block), :]
        row_pos = lax.broadcasted_iota(jnp.int32, (block, width), 0) + tile * block
        row_start = jnp.zeros((block, width), jnp.int32)
        for start in starts:
            row_start = jnp.where(row_pos >= start, start, row_start)
        row_pos = row_pos[:, :1]
        row_start = row_start[:, :1]
        lane_pos = lax.broadcasted_iota(jnp.int32, (block, block), 1)

        def score_step(at, top):
            key = all_key[pl.ds(pl.multiple_of(at * block, block), block), :]
            scores = lax.dot_general(
                query, key, (((1,), (1,)), ((), ())), preferred_element_type=jnp.float32
            ) * (1.0 / math.sqrt(HEAD_DIM))
            key_pos = lane_pos + at * block
            allowed = (key_pos <= row_pos) & (key_pos >= row_start)
            scores = jnp.where(allowed, scores, masked_score)
            score_buf[at - low] = scores
            for part in range(0, block, width):
                top = jnp.maximum(top, scores[:, part : part + width])
            return top

        top = lax.fori_loop(
            low, tile + 1, score_step, jnp.full((block, width), masked_score, jnp.float32)
        )
        top = jnp.max(top, axis=1, keepdims=True)

        def value_step(at, carried):
            running, weighted = carried
            value = all_value[pl.ds(pl.multiple_of(at * block, block), block), :]
            weight = jnp.exp(score_buf[at - low] - top)
            for part in range(0, block, width):
                running = running + weight[:, part : part + width]
            weighted = weighted + jnp.dot(
                weight.astype(jnp.bfloat16), value, preferred_element_type=jnp.float32
            )
            return (running, weighted)

        zero = jnp.zeros((block, width), jnp.float32)
        running, weighted = lax.fori_loop(low, tile + 1, value_step, (zero, zero))
        running = jnp.sum(running, axis=1, keepdims=True)
        attn_buf[pl.ds(row0, block), :] = (weighted / running).astype(jnp.bfloat16)

    def attn_send(step):
        peer = lax.rem(me + step, groups)
        sends[5, step] = remote(
            attn_buf.at[rows_of(peer), :], attn_ref.at[:, cols_of(me)], 5, step
        )
        sends[5, step].start()

    order = list(range(1, groups)) + [0]
    for place, step in enumerate(order):
        group = lax.rem(me + step, groups)

        def tile_body(at, carry, group=group):
            query_tile(group * per_row + at)
            return carry

        lax.fori_loop(0, per_row, tile_body, 0)
        if place > 0:
            attn_send(order[place - 1])

    arrive(4)

    def tap_body(at, carry):
        col0 = pl.multiple_of(at * block, block)
        tap_spec[at] = lax.dot_general(
            forward_ref[...],
            all_taps[:, pl.ds(col0, block)],
            (((1,), (1,)), ((), ())),
            preferred_element_type=jnp.float32,
        )
        return carry

    lax.fori_loop(0, blocks, tap_body, 0)
    own_attn = pltpu.make_async_copy(
        attn_buf.at[rows_of(me), :], attn_ref.at[:, cols_of(me)], local_sem.at[6]
    )
    own_attn.start()
    arrive(3)

    def signal_body(at, carry):
        row0 = pl.multiple_of(at * block, block)
        gated = all_gate[pl.ds(row0, block), :].astype(jnp.float32) * attn_buf[
            pl.ds(row0, block), :
        ].astype(jnp.float32)
        sig_spec[at] = jnp.dot(
            forward_ref[...], gated.astype(jnp.bfloat16), preferred_element_type=jnp.float32
        )
        return carry

    lax.fori_loop(0, blocks, signal_body, 0)

    lift = 8

    def product_body(at, carry):
        real = pl.ds(pl.multiple_of(at * lift, lift), lift)
        imag = pl.ds(pl.multiple_of(block + at * lift, lift), lift)
        odd = lax.rem(lax.broadcasted_iota(jnp.int32, (lift, width), 0), 2) == 1
        sign = jnp.where(odd, -1.0, 1.0).astype(jnp.float32)
        tap_real = []
        tap_imag = []
        for k in range(blocks):
            now_real = tap_spec[k, real, :]
            now_imag = tap_spec[k, imag, :]
            if k > 0:
                now_real = now_real - sign * tap_spec[k - 1, imag, :]
                now_imag = now_imag + sign * tap_spec[k - 1, real, :]
            tap_real.append(now_real)
            tap_imag.append(now_imag)
        for out in range(blocks):
            sum_real = jnp.zeros((lift, width), jnp.float32)
            sum_imag = jnp.zeros((lift, width), jnp.float32)
            for j in range(out + 1):
                sig_real = sig_spec[j, real, :]
                sig_imag = sig_spec[j, imag, :]
                sum_real = sum_real + sig_real * tap_real[out - j] - sig_imag * tap_imag[out - j]
                sum_imag = sum_imag + sig_real * tap_imag[out - j] + sig_imag * tap_real[out - j]
            prod_spec[out, real, :] = sum_real
            prod_spec[out, imag, :] = sum_imag
        return carry

    lax.fori_loop(0, block // lift, product_body, 0)

    def mixed_send(step):
        peer = lax.rem(me + step, groups)
        sends[6, step] = remote(
            mixed_buf.at[rows_of(peer), :], mixed_back.at[:, cols_of(me)], 6, step
        )
        sends[6, step].start()

    for place, step in enumerate(order):
        group = lax.rem(me + step, groups)

        def inverse_body(at, carry, group=group, step=step):
            index = group * per_row + at
            mixed = jnp.dot(
                inverse_ref[...],
                prod_spec[index].astype(jnp.bfloat16),
                preferred_element_type=jnp.float32,
            ).astype(jnp.bfloat16)
            if step == 0:
                mixed_back[pl.ds(pl.multiple_of(at * block, block), block), cols_of(me)] = mixed
            else:
                mixed_buf[pl.ds(pl.multiple_of(index * block, block), block), :] = mixed
            return carry

        lax.fori_loop(0, per_row, inverse_body, 0)
        if place > 0:
            mixed_send(order[place - 1])

    gate_copy.wait()
    for step in range(1, groups):
        sends[6, step].wait_recv()

    def final_body(at, carry):
        part = pl.ds(pl.multiple_of(at * 64, 64), 64)
        hyena_ref[part, :] = (
            own_out_gate[part, :].astype(jnp.float32) * mixed_back[part, :].astype(jnp.float32)
        ).astype(jnp.bfloat16)
        return carry

    lax.fori_loop(0, rows // 64, final_body, 0)
    own_attn.wait()
    for step in range(1, groups):
        sends[5, step].wait_recv()
    for copy in sends.values():
        copy.wait_send()


def fused_body(queries, key_rows, values, doc_lengths, in_gate, out_gate, filter_taps):
    rows, channels = queries.shape
    groups = lax.axis_size("ctx")
    width = channels // groups
    length = rows * groups
    block = BLOCK
    blocks = length // block
    reach = KV_REACH * (rows // block)
    forward, inverse = block_tables(block)
    anywhere = pl.BlockSpec(memory_space=pl.ANY)
    vmem = pl.BlockSpec(memory_space=pltpu.VMEM)
    half = jnp.bfloat16
    full = jnp.float32
    return pl.pallas_call(
        fused_kernel,
        out_shape=(
            jax.ShapeDtypeStruct((rows, channels), half),
            jax.ShapeDtypeStruct((rows, channels), half),
        ),
        in_specs=[pl.BlockSpec(memory_space=pltpu.SMEM)] + [anywhere] * 6 + [vmem] * 2,
        out_specs=(anywhere, vmem),
        scratch_shapes=[
            pltpu.VMEM((length, width), half),
            pltpu.VMEM((length, width), half),
            pltpu.VMEM((length, width), half),
            pltpu.VMEM((length, width), half),
            pltpu.VMEM((width, length), half),
            pltpu.VMEM((rows, channels), half),
            pltpu.VMEM((min(reach + 1, blocks), block, block), full),
            pltpu.VMEM((length, width), half),
            pltpu.VMEM((blocks, 2 * block, width), full),
            pltpu.VMEM((blocks, 2 * block, width), full),
            pltpu.VMEM((blocks, 2 * block, width), full),
            pltpu.VMEM((length, width), half),
            pltpu.VMEM((rows, channels), half),
            pltpu.SemaphoreType.DMA((7, groups)),
            pltpu.SemaphoreType.DMA((7, groups)),
            pltpu.SemaphoreType.DMA((7,)),
        ],
        compiler_params=pltpu.CompilerParams(
            collective_id=0, has_side_effects=True, vmem_limit_bytes=48 * 1024 * 1024
        ),
        name="fused_window",
    )(
        doc_lengths,
        queries,
        key_rows,
        values,
        in_gate,
        filter_taps.astype(half),
        out_gate,
        forward,
        inverse,
    )


def fits_fused(queries):
    rows, channels = queries.shape
    groups = lax.axis_size("ctx")
    return channels == groups * HEAD_DIM and rows % BLOCK == 0


def either_body(queries, *rest):
    if fits_fused(queries):
        return fused_body(queries, *rest)
    return body(queries, *rest)


def solution(mesh):
    return jax.shard_map(
        either_body,
        mesh=mesh,
        in_specs=(
            P(("dp", "ctx"), "tp"),
            P(("dp", "ctx"), "tp"),
            P(("dp", "ctx"), "tp"),
            P("dp"),
            P(("dp", "ctx"), "tp"),
            P(("dp", "ctx"), "tp"),
            P(("dp", "tp"), "ctx"),
        ),
        out_specs=(P(("dp", "ctx"), "tp"), P(("dp", "ctx"), "tp")),
        check_vma=False,
    )
```

```python
import math

import jax
import jax.numpy as jnp
import numpy as np
from jax import lax
from jax.experimental import pallas as pl
from jax.experimental.pallas import tpu as pltpu
from jax.sharding import PartitionSpec as P

HEAD_DIM = 128
KV_REACH = 3
BLOCK = 256


masked_score = -1e30


def passed_along(x, axis, by):
    length = lax.axis_size(axis)
    pairs = [(i, i + by) for i in range(length) if 0 <= i + by < length]
    return lax.ppermute(x, axis, pairs)


def doc_of(positions, doc_lengths):
    starts = jnp.cumsum(doc_lengths) - doc_lengths
    inside = (starts[None, :] <= positions[:, None]).astype(jnp.int32)
    return jnp.sum(inside, axis=1) - 1


def attend_block(carried, pair, query_heads, allowed):
    running_max, running_sum, weighted = carried
    row_count = query_heads.shape[0]
    key_heads = pair[0].reshape(row_count, -1, HEAD_DIM)
    value_heads = pair[1].reshape(row_count, -1, HEAD_DIM)
    scores = jnp.einsum(
        "qhd,khd->hqk", query_heads, key_heads, preferred_element_type=jnp.float32
    ) / math.sqrt(HEAD_DIM)
    scores = jnp.where(allowed[None], scores, masked_score)
    new_max = jnp.maximum(running_max, jnp.max(scores, axis=2))
    rescale = jnp.exp(running_max - new_max)
    exp_scores = jnp.exp(scores - new_max[:, :, None])
    running_sum = running_sum * rescale + jnp.sum(exp_scores, axis=2)
    weighted = weighted * rescale[:, :, None] + jnp.einsum(
        "hqk,khd->hqd",
        exp_scores.astype(jnp.bfloat16),
        value_heads,
        preferred_element_type=jnp.float32,
    )
    return (new_max, running_sum, weighted)


def split_parts(source):
    high_part = lax.optimization_barrier(source.astype(jnp.bfloat16))
    low_part = (source - high_part.astype(jnp.float32)).astype(jnp.bfloat16)
    return (high_part, low_part)


def split_mul(form, left_parts, right_parts):
    first = jnp.einsum(form, left_parts[0], right_parts[0], preferred_element_type=jnp.float32)
    second = jnp.einsum(form, left_parts[0], right_parts[1], preferred_element_type=jnp.float32)
    third = jnp.einsum(form, left_parts[1], right_parts[0], preferred_element_type=jnp.float32)
    return first + (second + third)


def dft_tables(length):
    inner_len = math.gcd(length, 256)
    outer_len = 2 * length // inner_len
    freq_rows = jnp.arange(outer_len, dtype=jnp.int32)
    time_rows = jnp.arange(outer_len // 2, dtype=jnp.int32)
    inner_index = jnp.arange(inner_len, dtype=jnp.int32)
    angle_outer = (
        2.0
        * math.pi
        / outer_len
        * (freq_rows[:, None] * time_rows[None, :] % outer_len).astype(jnp.float32)
    )
    angle_twist = (
        2.0
        * math.pi
        / (2 * length)
        * (freq_rows[:, None] * inner_index[None, :] % (2 * length)).astype(jnp.float32)
    )
    angle_inner = (
        2.0
        * math.pi
        / inner_len
        * (inner_index[:, None] * inner_index[None, :] % inner_len).astype(jnp.float32)
    )
    return (
        split_parts(jnp.cos(angle_outer)),
        split_parts(-jnp.sin(angle_outer)),
        jnp.cos(angle_twist),
        -jnp.sin(angle_twist),
        split_parts(jnp.cos(angle_inner)),
        split_parts(-jnp.sin(angle_inner)),
    )


def right_mul(left_parts, table_parts):
    return split_mul("cin,nm->cim", left_parts, table_parts)


def forward_dft(samples, tables):
    outer_cos, outer_sin, twist_cos, twist_sin, inner_cos, inner_sin = tables
    item_count = samples.shape[0]
    shaped = split_parts(samples.reshape(item_count, outer_cos[0].shape[1], inner_cos[0].shape[0]))
    section_real = split_mul("ij,cjn->cin", outer_cos, shaped)
    section_imag = split_mul("ij,cjn->cin", outer_sin, shaped)
    turned_real = split_parts(section_real * twist_cos - section_imag * twist_sin)
    turned_imag = split_parts(section_real * twist_sin + section_imag * twist_cos)
    spec_real = right_mul(turned_real, inner_cos) - right_mul(turned_imag, inner_sin)
    spec_imag = right_mul(turned_real, inner_sin) + right_mul(turned_imag, inner_cos)
    return (spec_real, spec_imag)


def inverse_dft(prod_real, prod_imag, tables):
    outer_cos, outer_sin, twist_cos, twist_sin, inner_cos, inner_sin = tables
    item_count = prod_real.shape[0]
    half_len = outer_cos[0].shape[1]
    inner_len = inner_cos[0].shape[0]
    real_parts = split_parts(prod_real)
    imag_parts = split_parts(prod_imag)
    back_real = right_mul(real_parts, inner_cos) + right_mul(imag_parts, inner_sin)
    back_imag = right_mul(imag_parts, inner_cos) - right_mul(real_parts, inner_sin)
    unturn_real = split_parts(back_real * twist_cos + back_imag * twist_sin)
    unturn_imag = split_parts(back_imag * twist_cos - back_real * twist_sin)
    rows_out = split_mul("ij,cin->cjn", outer_cos, unturn_real) + split_mul(
        "ij,cin->cjn", outer_sin, unturn_imag
    )
    return (rows_out * (1.0 / (2 * half_len * inner_len))).reshape(item_count, half_len * inner_len)


def filter_apply(signal, filter_spec, tables):
    sig_real, sig_imag = forward_dft(signal, tables)
    tap_real, tap_imag = filter_spec
    prod_real = sig_real * tap_real - sig_imag * tap_imag
    prod_imag = sig_real * tap_imag + sig_imag * tap_real
    return inverse_dft(prod_real, prod_imag, tables)


def body(queries, key_rows, values, doc_lengths, in_gate, out_gate, filter_taps):
    row_count, channels = queries.shape
    head_count = channels // HEAD_DIM
    group_count = lax.axis_size("ctx")
    per_group = channels // group_count
    seq_len = row_count * group_count
    tables = dft_tables(seq_len)
    taps_grouped = filter_taps.reshape(group_count, per_group, row_count)
    query_pos = lax.axis_index("ctx") * row_count + jnp.arange(row_count, dtype=jnp.int32)
    query_doc = doc_of(query_pos, doc_lengths)
    query_heads = queries.reshape(row_count, head_count, HEAD_DIM)
    carried = (
        jnp.full((head_count, row_count), masked_score, jnp.float32),
        jnp.zeros((head_count, row_count), jnp.float32),
        jnp.zeros((head_count, row_count, HEAD_DIM), jnp.float32),
    )

    def visit(state_now, pair, distance):
        key_pos = query_pos - distance * row_count
        key_doc = doc_of(key_pos, doc_lengths)
        allowed = (key_doc[None, :] == query_doc[:, None]) & (
            key_pos[None, :] <= query_pos[:, None]
        )
        return lax.cond(
            jnp.any(allowed),
            lambda state_in: attend_block(state_in, pair, query_heads, allowed),
            lambda state_in: state_in,
            state_now,
        )

    own_pair = jnp.stack((key_rows, values))
    carried = visit(carried, own_pair, 0)
    moving = own_pair
    for distance in range(1, KV_REACH + 1):
        moving = passed_along(moving, "ctx", 1)
        carried = visit(carried, moving, distance)
    running_max, running_sum, weighted = carried
    attended = (
        (weighted / running_sum[:, :, None])
        .transpose(1, 0, 2)
        .reshape(row_count, channels)
        .astype(jnp.bfloat16)
    )
    gated = (in_gate.astype(jnp.float32) * attended.astype(jnp.float32)).T
    gated_grouped = gated.reshape(group_count, per_group, row_count)
    pair = (
        lax.all_to_all(
            gated_grouped.astype(jnp.bfloat16), "ctx", split_axis=0, concat_axis=2, tiled=True
        ).astype(gated_grouped.dtype),
        lax.all_to_all(
            taps_grouped.astype(jnp.bfloat16), "ctx", split_axis=0, concat_axis=2, tiled=True
        ).astype(taps_grouped.dtype),
    )
    item_count = pair[0].shape[1]
    signal = pair[0].reshape(item_count, -1)
    taps = pair[1].reshape(item_count, -1)
    result = filter_apply(signal, forward_dft(taps, tables), tables)
    mixed = result.reshape(1, item_count, -1)
    returned = lax.all_to_all(
        mixed.astype(jnp.bfloat16), "ctx", split_axis=2, concat_axis=0, tiled=True
    ).astype(mixed.dtype)
    hyena_out = (out_gate.astype(jnp.float32) * returned.reshape(channels, row_count).T).astype(
        jnp.bfloat16
    )
    return (attended, hyena_out)


def block_tables(block):
    freq = np.arange(block)
    time = np.arange(block)
    angle = np.pi / (2 * block) * ((2 * freq[:, None] + 1) * time[None, :] % (4 * block))
    forward = np.concatenate((np.cos(angle), -np.sin(angle)), axis=0)
    inverse = forward.T / block
    return (jnp.asarray(forward, jnp.bfloat16), jnp.asarray(inverse, jnp.bfloat16))


def fused_kernel(
    docs_ref,
    query_ref,
    key_ref,
    value_ref,
    gate_ref,
    taps_ref,
    out_gate_ref,
    forward_ref,
    inverse_ref,
    attn_ref,
    hyena_ref,
    near_query,
    near_key,
    near_value,
    near_gate,
    near_attn,
    near_gated,
    wide_taps,
    half_taps,
    forward_buf,
    inverse_buf,
    all_query,
    all_key,
    all_value,
    all_gate,
    all_taps,
    own_out_gate,
    score_buf,
    attn_buf,
    sig_spec,
    tap_spec,
    prod_spec,
    mixed_buf,
    mixed_back,
    send_sem,
    recv_sem,
    local_sem,
    table_sem,
):
    rows, _ = query_ref.shape
    length, width = all_query.shape
    groups = length // rows
    block = inverse_ref.shape[0]
    half = groups // 2
    half_cols = pl.ds(half * width, width * (groups - half))
    blocks = length // block
    per_row = rows // block
    reach = KV_REACH * per_row
    me = lax.axis_index("ctx")
    lower = me < half

    def rows_of(group):
        return pl.ds(pl.multiple_of(group * rows, rows), rows)

    def cols_of(group):
        return pl.ds(pl.multiple_of(group * width, width), width)

    barrier = pltpu.get_barrier_semaphore()
    for step in range(1, groups):
        peer = lax.rem(me + step, groups)
        pl.semaphore_signal(
            barrier, inc=1, device_id={"ctx": peer}, device_id_type=pl.DeviceIdType.MESH
        )
    pl.semaphore_wait(barrier, groups - 1)

    class Later:
        def __init__(self, make):
            self.make = make

        def start(self):
            self.make().start()

        def wait(self):
            self.make().wait()

        def wait_recv(self):
            self.make().wait_recv()

        def wait_send(self):
            self.make().wait_send()

    def remote(refs, kind, step):
        def make():
            source, target = refs()
            return pltpu.make_async_remote_copy(
                src_ref=source,
                dst_ref=target,
                send_sem=send_sem.at[kind, step],
                recv_sem=recv_sem.at[kind, step],
                device_id={"ctx": lax.rem(me + step, groups)},
                device_id_type=pl.DeviceIdType.MESH,
            )

        return Later(make)

    def inbound(kind, step):
        peer = lax.rem(me + step, groups)
        source_of = (query_ref, key_ref, value_ref, gate_ref)
        target_of = (all_query, all_key, all_value, all_gate)
        if kind == 4:
            return (
                half_taps.at[cols_of(peer), :],
                all_taps.at[:, rows_of(me)],
            )
        return (source_of[kind].at[:, cols_of(peer)], target_of[kind].at[rows_of(me), :])

    def goes(kind, source, target):
        if kind == 0:
            return (source >= half) | (target < half)
        if kind == 5:
            return (source < half) | (target >= half)
        return None

    def guarded(condition, action):
        if condition is None:
            action()
        else:
            pl.when(condition)(action)

    sends = {}
    own = {}

    def make_send(kind, step):
        sends[kind, step] = remote(lambda: inbound(kind, step), kind, step)

    def near_copy(kind, step):
        source = (key_ref, value_ref)[kind - 7]
        target = (near_key, near_value)[kind - 7]
        return remote(
            lambda: (source.at[:, half_cols], target.at[rows_of(me), :]), kind, step
        )

    def own_copy(refs, place):
        def make():
            source, target = refs()
            return pltpu.make_async_copy(source, target, table_sem.at[place])

        own[place] = Later(make)
        own[place].start()

    for kind in (7, 8):
        for step in range(1, half):
            sends[kind, step] = near_copy(kind, step)
            pl.when(me + step < half)(sends[kind, step].start)
    for kind in range(4):
        for step in range(1, groups):
            make_send(kind, step)
            peer = lax.rem(me + step, groups)
            guarded(
                goes(0, me, peer) if kind in (0, 3) else None, sends[kind, step].start
            )

    @pl.when(lower)
    def _():
        own_copy(lambda: (query_ref.at[:, half_cols], near_query), 0)
        own_copy(lambda: (key_ref.at[:, half_cols], near_key.at[rows_of(me), :]), 1)
        own_copy(lambda: (value_ref.at[:, half_cols], near_value.at[rows_of(me), :]), 2)
        own_copy(lambda: (gate_ref.at[:, half_cols], near_gate), 3)

    own_copy(lambda: (taps_ref, wide_taps), 4)
    own_copy(lambda: (forward_ref, forward_buf), 5)
    own_copy(lambda: (inverse_ref, inverse_buf), 6)
    local = {}
    for kind in range(4):
        source, target = inbound(kind, 0)
        local[kind] = pltpu.make_async_copy(source, target, local_sem.at[kind])
        local[kind].start()
    gate_copy = pltpu.make_async_copy(out_gate_ref, own_out_gate, local_sem.at[5])
    gate_copy.start()

    def arrive(kind):
        local[kind].wait()
        for step in range(1, groups):
            source = lax.rem(me + groups - step, groups)
            guarded(goes(kind, source, me), sends[kind, step].wait_recv)

    starts = []
    total = 0
    for doc in range(docs_ref.shape[0]):
        starts.append(total)
        total = total + docs_ref[doc]

    def query_tile(tile, query, key_of, value_of):
        low = jnp.maximum(tile - reach, 0)
        row_pos = lax.broadcasted_iota(jnp.int32, (block, width), 0) + tile * block
        row_start = jnp.zeros((block, width), jnp.int32)
        for start in starts:
            row_start = jnp.where(row_pos >= start, start, row_start)
        row_pos = row_pos[:, :1]
        row_start = row_start[:, :1]
        lane_pos = lax.broadcasted_iota(jnp.int32, (block, block), 1)

        def score_step(at, top):
            key = key_of(pl.ds(pl.multiple_of(at * block, block), block))
            scores = lax.dot_general(
                query, key, (((1,), (1,)), ((), ())), preferred_element_type=jnp.float32
            ) * (1.0 / math.sqrt(HEAD_DIM))
            key_pos = lane_pos + at * block
            allowed = (key_pos <= row_pos) & (key_pos >= row_start)
            scores = jnp.where(allowed, scores, masked_score)
            score_buf[at - low] = scores
            for part in range(0, block, width):
                top = jnp.maximum(top, scores[:, part : part + width])
            return top

        top = lax.fori_loop(
            low, tile + 1, score_step, jnp.full((block, width), masked_score, jnp.float32)
        )
        top = jnp.max(top, axis=1, keepdims=True)

        def value_step(at, carried):
            running, weighted = carried
            value = value_of(pl.ds(pl.multiple_of(at * block, block), block))
            weight = jnp.exp(score_buf[at - low] - top)
            for part in range(0, block, width):
                running = running + weight[:, part : part + width]
            weighted = weighted + jnp.dot(
                weight.astype(jnp.bfloat16), value, preferred_element_type=jnp.float32
            )
            return (running, weighted)

        zero = jnp.zeros((block, width), jnp.float32)
        running, weighted = lax.fori_loop(low, tile + 1, value_step, (zero, zero))
        running = jnp.sum(running, axis=1, keepdims=True)
        return (weighted / running).astype(jnp.bfloat16)

    def near_send(head):
        for step in range(1, groups):
            peer = lax.rem(me + step, groups)

            @pl.when(lower & (peer == half + head))
            def _(step=step):
                remote(
                    lambda: (
                        near_gated.at[:, pl.ds(head * width, width)],
                        all_gate.at[rows_of(me), :],
                    ),
                    3,
                    step,
                ).start()

    @pl.when(lower)
    def _():
        for place in range(4):
            own[place].wait()
        for kind in (7, 8):
            for step in range(1, half):
                pl.when(me - step >= 0)(sends[kind, step].wait_recv)
        for head in range(groups - half):
            cols = pl.ds(head * width, width)

            def near_body(at, carry, cols=cols):
                part = pl.ds(pl.multiple_of(at * block, block), block)
                attended = query_tile(
                    me * per_row + at,
                    near_query[part, cols],
                    lambda rows_at: near_key[rows_at, cols],
                    lambda rows_at: near_value[rows_at, cols],
                )
                near_attn[part, cols] = attended
                near_gated[part, cols] = (
                    near_gate[part, cols].astype(jnp.float32) * attended.astype(jnp.float32)
                ).astype(jnp.bfloat16)
                return carry

            lax.fori_loop(0, per_row, near_body, 0)
            if head > 0:
                near_send(head - 1)

    own[4].wait()

    def round_body(at, carry):
        part = pl.ds(pl.multiple_of(at * 64, 64), 64)
        half_taps[part, :] = wide_taps[part, :].astype(jnp.bfloat16)
        return carry

    lax.fori_loop(0, half_taps.shape[0] // 64, round_body, 0)
    near_send(groups - half - 1)
    near_out = Later(
        lambda: pltpu.make_async_copy(near_attn, attn_ref.at[:, half_cols], table_sem.at[7])
    )
    pl.when(lower)(near_out.start)

    arrive(0)
    for step in range(1, groups):
        make_send(4, step)
        sends[4, step].start()
    source, target = inbound(4, 0)
    local[4] = pltpu.make_async_copy(source, target, local_sem.at[4])
    local[4].start()
    arrive(1)
    arrive(2)

    def attn_send(step):
        peer = lax.rem(me + step, groups)
        sends[5, step] = remote(
            lambda: (attn_buf.at[rows_of(peer), :], attn_ref.at[:, cols_of(me)]), 5, step
        )
        guarded(goes(5, me, peer), sends[5, step].start)

    order = list(range(1, groups)) + [0]
    for place, step in enumerate(order):
        group = lax.rem(me + step, groups)

        def tile_body(at, carry, group=group):
            tile = group * per_row + at
            part = pl.ds(pl.multiple_of(tile * block, block), block)
            attn_buf[part, :] = query_tile(
                tile,
                all_query[part, :],
                lambda rows_at: all_key[rows_at, :],
                lambda rows_at: all_value[rows_at, :],
            )
            return carry

        @pl.when(goes(5, me, group))
        def _(tile_body=tile_body):
            lax.fori_loop(0, per_row, tile_body, 0)

        if place > 0:
            attn_send(order[place - 1])

    arrive(4)
    own[5].wait()
    own[6].wait()

    def tap_body(at, carry):
        col0 = pl.multiple_of(at * block, block)
        tap_spec[at] = lax.dot_general(
            forward_buf[...],
            all_taps[:, pl.ds(col0, block)],
            (((1,), (1,)), ((), ())),
            preferred_element_type=jnp.float32,
        )
        return carry

    lax.fori_loop(0, blocks, tap_body, 0)
    own_attn = pltpu.make_async_copy(
        attn_buf.at[rows_of(me), :], attn_ref.at[:, cols_of(me)], local_sem.at[6]
    )
    own_attn.start()
    arrive(3)

    def signal_body(at, carry):
        row0 = pl.multiple_of(at * block, block)
        arrived = all_gate[pl.ds(row0, block), :]
        gated = arrived.astype(jnp.float32) * attn_buf[pl.ds(row0, block), :].astype(jnp.float32)
        ready = (me >= half) & (at < half * per_row)
        gated = jnp.where(ready, arrived, gated.astype(jnp.bfloat16))
        sig_spec[at] = jnp.dot(forward_buf[...], gated, preferred_element_type=jnp.float32)
        return carry

    lax.fori_loop(0, blocks, signal_body, 0)

    lift = 8

    def product_body(at, carry):
        real = pl.ds(pl.multiple_of(at * lift, lift), lift)
        imag = pl.ds(pl.multiple_of(block + at * lift, lift), lift)
        odd = lax.rem(lax.broadcasted_iota(jnp.int32, (lift, width), 0), 2) == 1
        sign = jnp.where(odd, -1.0, 1.0).astype(jnp.float32)
        tap_real = []
        tap_imag = []
        for k in range(blocks):
            now_real = tap_spec[k, real, :]
            now_imag = tap_spec[k, imag, :]
            if k > 0:
                now_real = now_real - sign * tap_spec[k - 1, imag, :]
                now_imag = now_imag + sign * tap_spec[k - 1, real, :]
            tap_real.append(now_real)
            tap_imag.append(now_imag)
        for out in range(blocks):
            sum_real = jnp.zeros((lift, width), jnp.float32)
            sum_imag = jnp.zeros((lift, width), jnp.float32)
            for j in range(out + 1):
                sig_real = sig_spec[j, real, :]
                sig_imag = sig_spec[j, imag, :]
                sum_real = sum_real + sig_real * tap_real[out - j] - sig_imag * tap_imag[out - j]
                sum_imag = sum_imag + sig_real * tap_imag[out - j] + sig_imag * tap_real[out - j]
            prod_spec[out, real, :] = sum_real
            prod_spec[out, imag, :] = sum_imag
        return carry

    lax.fori_loop(0, block // lift, product_body, 0)

    def mixed_send(step):
        peer = lax.rem(me + step, groups)
        sends[6, step] = remote(
            lambda: (mixed_buf.at[rows_of(peer), :], mixed_back.at[:, cols_of(me)]), 6, step
        )
        sends[6, step].start()

    for place, step in enumerate(order):
        group = lax.rem(me + step, groups)

        def inverse_body(at, carry, group=group, step=step):
            index = group * per_row + at
            mixed = jnp.dot(
                inverse_buf[...],
                prod_spec[index].astype(jnp.bfloat16),
                preferred_element_type=jnp.float32,
            ).astype(jnp.bfloat16)
            if step == 0:
                mixed_back[pl.ds(pl.multiple_of(at * block, block), block), cols_of(me)] = mixed
            else:
                mixed_buf[pl.ds(pl.multiple_of(index * block, block), block), :] = mixed
            return carry

        lax.fori_loop(0, per_row, inverse_body, 0)
        if place > 0:
            mixed_send(order[place - 1])

    gate_copy.wait()
    for step in range(1, groups):
        sends[6, step].wait_recv()

    def final_body(at, carry):
        part = pl.ds(pl.multiple_of(at * 64, 64), 64)
        hyena_ref[part, :] = (
            own_out_gate[part, :].astype(jnp.float32) * mixed_back[part, :].astype(jnp.float32)
        ).astype(jnp.bfloat16)
        return carry

    lax.fori_loop(0, rows // 64, final_body, 0)
    own_attn.wait()
    pl.when(lower)(near_out.wait)
    for step in range(1, groups):
        source = lax.rem(me + groups - step, groups)
        guarded(goes(5, source, me), sends[5, step].wait_recv)
    for (kind, step), copy in sends.items():
        if kind >= 7:
            guarded(me + step < half, copy.wait_send)
        else:
            guarded(goes(kind, me, lax.rem(me + step, groups)), copy.wait_send)


def fused_body(queries, key_rows, values, doc_lengths, in_gate, out_gate, filter_taps):
    rows, channels = queries.shape
    groups = lax.axis_size("ctx")
    width = channels // groups
    length = rows * groups
    block = BLOCK
    blocks = length // block
    reach = KV_REACH * (rows // block)
    forward, inverse = block_tables(block)
    near = groups // 2
    far = (groups - near) * width
    anywhere = pl.BlockSpec(memory_space=pl.ANY)
    vmem = pl.BlockSpec(memory_space=pltpu.VMEM)
    half = jnp.bfloat16
    full = jnp.float32
    return pl.pallas_call(
        fused_kernel,
        out_shape=(
            jax.ShapeDtypeStruct((rows, channels), half),
            jax.ShapeDtypeStruct((rows, channels), half),
        ),
        in_specs=[pl.BlockSpec(memory_space=pltpu.SMEM)] + [anywhere] * 8,
        out_specs=(anywhere, vmem),
        scratch_shapes=[
            pltpu.VMEM((rows, far), half),
            pltpu.VMEM((near * rows, far), half),
            pltpu.VMEM((near * rows, far), half),
            pltpu.VMEM((rows, far), half),
            pltpu.VMEM((rows, far), half),
            pltpu.VMEM((rows, far), half),
            pltpu.VMEM(filter_taps.shape, full),
            pltpu.VMEM(filter_taps.shape, half),
            pltpu.VMEM(forward.shape, half),
            pltpu.VMEM(inverse.shape, half),
            pltpu.VMEM((length, width), half),
            pltpu.VMEM((length, width), half),
            pltpu.VMEM((length, width), half),
            pltpu.VMEM((length, width), half),
            pltpu.VMEM((width, length), half),
            pltpu.VMEM((rows, channels), half),
            pltpu.VMEM((min(reach + 1, blocks), block, block), full),
            pltpu.VMEM((length, width), half),
            pltpu.VMEM((blocks, 2 * block, width), full),
            pltpu.VMEM((blocks, 2 * block, width), full),
            pltpu.VMEM((blocks, 2 * block, width), full),
            pltpu.VMEM((length, width), half),
            pltpu.VMEM((rows, channels), half),
            pltpu.SemaphoreType.DMA((9, groups)),
            pltpu.SemaphoreType.DMA((9, groups)),
            pltpu.SemaphoreType.DMA((7,)),
            pltpu.SemaphoreType.DMA((8,)),
        ],
        compiler_params=pltpu.CompilerParams(
            collective_id=0, has_side_effects=True, vmem_limit_bytes=67043328
        ),
        name="fused_window",
    )(
        doc_lengths,
        queries,
        key_rows,
        values,
        in_gate,
        filter_taps,
        out_gate,
        forward,
        inverse,
    )


def fits_fused(queries):
    rows, channels = queries.shape
    groups = lax.axis_size("ctx")
    return channels == groups * HEAD_DIM and rows % BLOCK == 0


def either_body(queries, *rest):
    if fits_fused(queries):
        return fused_body(queries, *rest)
    return body(queries, *rest)


def solution(mesh):
    return jax.shard_map(
        either_body,
        mesh=mesh,
        in_specs=(
            P(("dp", "ctx"), "tp"),
            P(("dp", "ctx"), "tp"),
            P(("dp", "ctx"), "tp"),
            P("dp"),
            P(("dp", "ctx"), "tp"),
            P(("dp", "ctx"), "tp"),
            P(("dp", "tp"), "ctx"),
        ),
        out_specs=(P(("dp", "ctx"), "tp"), P(("dp", "ctx"), "tp")),
        check_vma=False,
    )
```

```python
import math

import jax
import jax.numpy as jnp
import numpy as np
from jax import lax
from jax.experimental import pallas as pl
from jax.experimental.pallas import tpu as pltpu
from jax.sharding import PartitionSpec as P

HEAD_DIM = 128
KV_REACH = 3
BLOCK = 256


masked_score = -1e30


def passed_along(x, axis, by):
    length = lax.axis_size(axis)
    pairs = [(i, i + by) for i in range(length) if 0 <= i + by < length]
    return lax.ppermute(x, axis, pairs)


def doc_of(positions, doc_lengths):
    starts = jnp.cumsum(doc_lengths) - doc_lengths
    inside = (starts[None, :] <= positions[:, None]).astype(jnp.int32)
    return jnp.sum(inside, axis=1) - 1


def attend_block(carried, pair, query_heads, allowed):
    running_max, running_sum, weighted = carried
    row_count = query_heads.shape[0]
    key_heads = pair[0].reshape(row_count, -1, HEAD_DIM)
    value_heads = pair[1].reshape(row_count, -1, HEAD_DIM)
    scores = jnp.einsum(
        "qhd,khd->hqk", query_heads, key_heads, preferred_element_type=jnp.float32
    ) / math.sqrt(HEAD_DIM)
    scores = jnp.where(allowed[None], scores, masked_score)
    new_max = jnp.maximum(running_max, jnp.max(scores, axis=2))
    rescale = jnp.exp(running_max - new_max)
    exp_scores = jnp.exp(scores - new_max[:, :, None])
    running_sum = running_sum * rescale + jnp.sum(exp_scores, axis=2)
    weighted = weighted * rescale[:, :, None] + jnp.einsum(
        "hqk,khd->hqd",
        exp_scores.astype(jnp.bfloat16),
        value_heads,
        preferred_element_type=jnp.float32,
    )
    return (new_max, running_sum, weighted)


def split_parts(source):
    high_part = lax.optimization_barrier(source.astype(jnp.bfloat16))
    low_part = (source - high_part.astype(jnp.float32)).astype(jnp.bfloat16)
    return (high_part, low_part)


def split_mul(form, left_parts, right_parts):
    first = jnp.einsum(form, left_parts[0], right_parts[0], preferred_element_type=jnp.float32)
    second = jnp.einsum(form, left_parts[0], right_parts[1], preferred_element_type=jnp.float32)
    third = jnp.einsum(form, left_parts[1], right_parts[0], preferred_element_type=jnp.float32)
    return first + (second + third)


def dft_tables(length):
    inner_len = math.gcd(length, 256)
    outer_len = 2 * length // inner_len
    freq_rows = jnp.arange(outer_len, dtype=jnp.int32)
    time_rows = jnp.arange(outer_len // 2, dtype=jnp.int32)
    inner_index = jnp.arange(inner_len, dtype=jnp.int32)
    angle_outer = (
        2.0
        * math.pi
        / outer_len
        * (freq_rows[:, None] * time_rows[None, :] % outer_len).astype(jnp.float32)
    )
    angle_twist = (
        2.0
        * math.pi
        / (2 * length)
        * (freq_rows[:, None] * inner_index[None, :] % (2 * length)).astype(jnp.float32)
    )
    angle_inner = (
        2.0
        * math.pi
        / inner_len
        * (inner_index[:, None] * inner_index[None, :] % inner_len).astype(jnp.float32)
    )
    return (
        split_parts(jnp.cos(angle_outer)),
        split_parts(-jnp.sin(angle_outer)),
        jnp.cos(angle_twist),
        -jnp.sin(angle_twist),
        split_parts(jnp.cos(angle_inner)),
        split_parts(-jnp.sin(angle_inner)),
    )


def right_mul(left_parts, table_parts):
    return split_mul("cin,nm->cim", left_parts, table_parts)


def forward_dft(samples, tables):
    outer_cos, outer_sin, twist_cos, twist_sin, inner_cos, inner_sin = tables
    item_count = samples.shape[0]
    shaped = split_parts(samples.reshape(item_count, outer_cos[0].shape[1], inner_cos[0].shape[0]))
    section_real = split_mul("ij,cjn->cin", outer_cos, shaped)
    section_imag = split_mul("ij,cjn->cin", outer_sin, shaped)
    turned_real = split_parts(section_real * twist_cos - section_imag * twist_sin)
    turned_imag = split_parts(section_real * twist_sin + section_imag * twist_cos)
    spec_real = right_mul(turned_real, inner_cos) - right_mul(turned_imag, inner_sin)
    spec_imag = right_mul(turned_real, inner_sin) + right_mul(turned_imag, inner_cos)
    return (spec_real, spec_imag)


def inverse_dft(prod_real, prod_imag, tables):
    outer_cos, outer_sin, twist_cos, twist_sin, inner_cos, inner_sin = tables
    item_count = prod_real.shape[0]
    half_len = outer_cos[0].shape[1]
    inner_len = inner_cos[0].shape[0]
    real_parts = split_parts(prod_real)
    imag_parts = split_parts(prod_imag)
    back_real = right_mul(real_parts, inner_cos) + right_mul(imag_parts, inner_sin)
    back_imag = right_mul(imag_parts, inner_cos) - right_mul(real_parts, inner_sin)
    unturn_real = split_parts(back_real * twist_cos + back_imag * twist_sin)
    unturn_imag = split_parts(back_imag * twist_cos - back_real * twist_sin)
    rows_out = split_mul("ij,cin->cjn", outer_cos, unturn_real) + split_mul(
        "ij,cin->cjn", outer_sin, unturn_imag
    )
    return (rows_out * (1.0 / (2 * half_len * inner_len))).reshape(item_count, half_len * inner_len)


def filter_apply(signal, filter_spec, tables):
    sig_real, sig_imag = forward_dft(signal, tables)
    tap_real, tap_imag = filter_spec
    prod_real = sig_real * tap_real - sig_imag * tap_imag
    prod_imag = sig_real * tap_imag + sig_imag * tap_real
    return inverse_dft(prod_real, prod_imag, tables)


def body(queries, key_rows, values, doc_lengths, in_gate, out_gate, filter_taps):
    row_count, channels = queries.shape
    head_count = channels // HEAD_DIM
    group_count = lax.axis_size("ctx")
    per_group = channels // group_count
    seq_len = row_count * group_count
    tables = dft_tables(seq_len)
    taps_grouped = filter_taps.reshape(group_count, per_group, row_count)
    query_pos = lax.axis_index("ctx") * row_count + jnp.arange(row_count, dtype=jnp.int32)
    query_doc = doc_of(query_pos, doc_lengths)
    query_heads = queries.reshape(row_count, head_count, HEAD_DIM)
    carried = (
        jnp.full((head_count, row_count), masked_score, jnp.float32),
        jnp.zeros((head_count, row_count), jnp.float32),
        jnp.zeros((head_count, row_count, HEAD_DIM), jnp.float32),
    )

    def visit(state_now, pair, distance):
        key_pos = query_pos - distance * row_count
        key_doc = doc_of(key_pos, doc_lengths)
        allowed = (key_doc[None, :] == query_doc[:, None]) & (
            key_pos[None, :] <= query_pos[:, None]
        )
        return lax.cond(
            jnp.any(allowed),
            lambda state_in: attend_block(state_in, pair, query_heads, allowed),
            lambda state_in: state_in,
            state_now,
        )

    own_pair = jnp.stack((key_rows, values))
    carried = visit(carried, own_pair, 0)
    moving = own_pair
    for distance in range(1, KV_REACH + 1):
        moving = passed_along(moving, "ctx", 1)
        carried = visit(carried, moving, distance)
    running_max, running_sum, weighted = carried
    attended = (
        (weighted / running_sum[:, :, None])
        .transpose(1, 0, 2)
        .reshape(row_count, channels)
        .astype(jnp.bfloat16)
    )
    gated = (in_gate.astype(jnp.float32) * attended.astype(jnp.float32)).T
    gated_grouped = gated.reshape(group_count, per_group, row_count)
    pair = (
        lax.all_to_all(
            gated_grouped.astype(jnp.bfloat16), "ctx", split_axis=0, concat_axis=2, tiled=True
        ).astype(gated_grouped.dtype),
        lax.all_to_all(
            taps_grouped.astype(jnp.bfloat16), "ctx", split_axis=0, concat_axis=2, tiled=True
        ).astype(taps_grouped.dtype),
    )
    item_count = pair[0].shape[1]
    signal = pair[0].reshape(item_count, -1)
    taps = pair[1].reshape(item_count, -1)
    result = filter_apply(signal, forward_dft(taps, tables), tables)
    mixed = result.reshape(1, item_count, -1)
    returned = lax.all_to_all(
        mixed.astype(jnp.bfloat16), "ctx", split_axis=2, concat_axis=0, tiled=True
    ).astype(mixed.dtype)
    hyena_out = (out_gate.astype(jnp.float32) * returned.reshape(channels, row_count).T).astype(
        jnp.bfloat16
    )
    return (attended, hyena_out)


def block_tables(block):
    freq = np.arange(block)
    time = np.arange(block)
    angle = np.pi / (2 * block) * ((2 * freq[:, None] + 1) * time[None, :] % (4 * block))
    forward = np.concatenate((np.cos(angle), -np.sin(angle)), axis=0)
    inverse = forward.T / block
    return (jnp.asarray(forward, jnp.bfloat16), jnp.asarray(inverse, jnp.bfloat16))


def fused_kernel(
    docs_ref,
    query_ref,
    key_ref,
    value_ref,
    gate_ref,
    taps_ref,
    forward_ref,
    inverse_ref,
    attn_ref,
    mixed_back,
    near_query,
    near_key,
    near_value,
    near_gate,
    near_attn,
    near_gated,
    wide_taps,
    half_taps,
    forward_buf,
    inverse_buf,
    all_query,
    all_key,
    all_value,
    all_gate,
    all_taps,
    score_buf,
    attn_buf,
    sig_spec,
    tap_spec,
    prod_spec,
    mixed_buf,
    send_sem,
    recv_sem,
    local_sem,
    table_sem,
):
    rows, _ = query_ref.shape
    length, width = all_query.shape
    groups = length // rows
    block = inverse_ref.shape[0]
    half = groups // 2
    half_cols = pl.ds(half * width, width * (groups - half))
    blocks = length // block
    per_row = rows // block
    me = lax.axis_index("ctx")
    lower = me < half

    def rows_of(group):
        return pl.ds(pl.multiple_of(group * rows, rows), rows)

    def cols_of(group):
        return pl.ds(pl.multiple_of(group * width, width), width)

    barrier = pltpu.get_barrier_semaphore()
    for step in range(1, groups):
        peer = lax.rem(me + step, groups)
        pl.semaphore_signal(
            barrier, inc=1, device_id={"ctx": peer}, device_id_type=pl.DeviceIdType.MESH
        )
    pl.semaphore_wait(barrier, groups - 1)

    class Later:
        def __init__(self, make):
            self.make = make

        def start(self):
            self.make().start()

        def wait(self):
            self.make().wait()

        def wait_recv(self):
            self.make().wait_recv()

        def wait_send(self):
            self.make().wait_send()

    def remote(refs, kind, step):
        def make():
            source, target = refs()
            return pltpu.make_async_remote_copy(
                src_ref=source,
                dst_ref=target,
                send_sem=send_sem.at[kind, step],
                recv_sem=recv_sem.at[kind, step],
                device_id={"ctx": lax.rem(me + step, groups)},
                device_id_type=pl.DeviceIdType.MESH,
            )

        return Later(make)

    def inbound(kind, step):
        peer = lax.rem(me + step, groups)
        source_of = (query_ref, key_ref, value_ref, gate_ref)
        target_of = (all_query, all_key, all_value, all_gate)
        if kind == 4:
            return (
                half_taps.at[cols_of(peer), :],
                all_taps.at[:, rows_of(me)],
            )
        return (source_of[kind].at[:, cols_of(peer)], target_of[kind].at[rows_of(me), :])

    def goes(kind, source, target):
        if kind == 0:
            return (source >= half) | (target < half)
        if kind == 5:
            return (source < half) | (target >= half)
        return None

    def guarded(condition, action):
        if condition is None:
            action()
        else:
            pl.when(condition)(action)

    sends = {}
    own = {}

    def make_send(kind, step):
        sends[kind, step] = remote(lambda: inbound(kind, step), kind, step)

    def near_copy(kind, step):
        source = (key_ref, value_ref)[kind - 7]
        target = (near_key, near_value)[kind - 7]
        return remote(
            lambda: (source.at[:, half_cols], target.at[rows_of(me), :]), kind, step
        )

    def own_copy(refs, place):
        def make():
            source, target = refs()
            return pltpu.make_async_copy(source, target, table_sem.at[place])

        own[place] = Later(make)
        own[place].start()

    for kind in (7, 8):
        for step in range(1, half):
            sends[kind, step] = near_copy(kind, step)
            pl.when(me + step < half)(sends[kind, step].start)
    for kind in range(4):
        for step in range(1, groups):
            make_send(kind, step)
            peer = lax.rem(me + step, groups)
            guarded(
                goes(0, me, peer) if kind in (0, 3) else None, sends[kind, step].start
            )

    @pl.when(lower)
    def _():
        own_copy(lambda: (query_ref.at[:, half_cols], near_query), 0)
        own_copy(lambda: (key_ref.at[:, half_cols], near_key.at[rows_of(me), :]), 1)
        own_copy(lambda: (value_ref.at[:, half_cols], near_value.at[rows_of(me), :]), 2)
        own_copy(lambda: (gate_ref.at[:, half_cols], near_gate), 3)

    own_copy(lambda: (taps_ref, wide_taps), 4)
    own_copy(lambda: (forward_ref, forward_buf), 5)
    own_copy(lambda: (inverse_ref, inverse_buf), 6)
    local = {}
    for kind in range(4):
        source, target = inbound(kind, 0)
        local[kind] = pltpu.make_async_copy(source, target, local_sem.at[kind])
        local[kind].start()

    def arrive(kind):
        local[kind].wait()
        for step in range(1, groups):
            source = lax.rem(me + groups - step, groups)
            guarded(goes(kind, source, me), sends[kind, step].wait_recv)

    starts = []
    total = 0
    for doc in range(docs_ref.shape[0]):
        starts.append(total)
        total = total + docs_ref[doc]

    def query_tile(group, at, query, key_of, value_of):
        first = jnp.maximum(group - KV_REACH, 0)
        row_pos = lax.broadcasted_iota(jnp.int32, (block, width), 0) + (group * rows + at * block)
        row_start = jnp.zeros((block, width), jnp.int32)
        for start in starts:
            row_start = jnp.where(row_pos >= start, start, row_start)
        row_pos = row_pos[:, :1]
        row_start = row_start[:, :1]
        lane_pos = lax.broadcasted_iota(jnp.int32, (block, rows), 1)

        def score_step(chunk, top, last=False):
            scores = lax.dot_general(
                query,
                key_of(rows_of(chunk)),
                (((1,), (1,)), ((), ())),
                preferred_element_type=jnp.float32,
            )
            allowed = lane_pos >= row_start - chunk * rows
            if last:
                allowed = allowed & (lane_pos <= row_pos - chunk * rows)
            scores = jnp.where(allowed, scores, masked_score)
            score_buf[chunk - first] = scores
            for part in range(0, rows, width):
                top = jnp.maximum(top, scores[:, part : part + width])
            return top

        top = jnp.full((block, width), masked_score, jnp.float32)
        top = lax.fori_loop(first, group, score_step, top)
        top = score_step(group, top, last=True)
        top = jnp.max(top, axis=1, keepdims=True)

        def value_step(chunk, carried):
            running, weighted = carried
            weight = jnp.exp2(
                (score_buf[chunk - first] - top) * (math.log2(math.e) / math.sqrt(HEAD_DIM))
            )
            for part in range(0, rows, width):
                running = running + weight[:, part : part + width]
            weighted = weighted + jnp.dot(
                weight.astype(jnp.bfloat16),
                value_of(rows_of(chunk)),
                preferred_element_type=jnp.float32,
            )
            return (running, weighted)

        zero = jnp.zeros((block, width), jnp.float32)
        running, weighted = lax.fori_loop(first, group + 1, value_step, (zero, zero))
        running = jnp.sum(running, axis=1, keepdims=True)
        return (weighted / running).astype(jnp.bfloat16)

    def near_send(head):
        for step in range(1, groups):
            peer = lax.rem(me + step, groups)

            @pl.when(lower & (peer == half + head))
            def _(step=step):
                remote(
                    lambda: (
                        near_gated.at[:, pl.ds(head * width, width)],
                        all_gate.at[rows_of(me), :],
                    ),
                    3,
                    step,
                ).start()

    @pl.when(lower)
    def _():
        for place in range(4):
            own[place].wait()
        for kind in (7, 8):
            for step in range(1, half):
                pl.when(me - step >= 0)(sends[kind, step].wait_recv)
        for head in range(groups - half):
            cols = pl.ds(head * width, width)

            def near_body(at, carry, cols=cols):
                part = pl.ds(pl.multiple_of(at * block, block), block)
                attended = query_tile(
                    me,
                    at,
                    near_query[part, cols],
                    lambda rows_at: near_key[rows_at, cols],
                    lambda rows_at: near_value[rows_at, cols],
                )
                near_attn[part, cols] = attended
                near_gated[part, cols] = (
                    near_gate[part, cols].astype(jnp.float32) * attended.astype(jnp.float32)
                ).astype(jnp.bfloat16)
                return carry

            lax.fori_loop(0, per_row, near_body, 0)
            if head > 0:
                near_send(head - 1)

    own[4].wait()

    def round_body(at, carry):
        part = pl.ds(pl.multiple_of(at * 64, 64), 64)
        half_taps[part, :] = wide_taps[part, :].astype(jnp.bfloat16)
        return carry

    lax.fori_loop(0, half_taps.shape[0] // 64, round_body, 0)
    near_send(groups - half - 1)
    near_out = Later(
        lambda: pltpu.make_async_copy(near_attn, attn_ref.at[:, half_cols], table_sem.at[7])
    )
    pl.when(lower)(near_out.start)

    arrive(0)
    for step in range(1, groups):
        make_send(4, step)
        sends[4, step].start()
    source, target = inbound(4, 0)
    local[4] = pltpu.make_async_copy(source, target, local_sem.at[4])
    local[4].start()
    arrive(1)
    arrive(2)

    def attn_send(step):
        peer = lax.rem(me + step, groups)
        sends[5, step] = remote(
            lambda: (attn_buf.at[rows_of(peer), :], attn_ref.at[:, cols_of(me)]), 5, step
        )
        guarded(goes(5, me, peer), sends[5, step].start)

    order = list(range(1, groups)) + [0]
    for place, step in enumerate(order):
        group = lax.rem(me + step, groups)

        def tile_body(at, carry, group=group):
            tile = group * per_row + at
            part = pl.ds(pl.multiple_of(tile * block, block), block)
            attn_buf[part, :] = query_tile(
                group,
                at,
                all_query[part, :],
                lambda rows_at: all_key[rows_at, :],
                lambda rows_at: all_value[rows_at, :],
            )
            return carry

        @pl.when(goes(5, me, group))
        def _(tile_body=tile_body):
            lax.fori_loop(0, per_row, tile_body, 0)

        if place > 0:
            attn_send(order[place - 1])

    arrive(4)
    own[5].wait()
    own[6].wait()

    def tap_body(at, carry):
        col0 = pl.multiple_of(at * block, block)
        tap_spec[at] = lax.dot_general(
            forward_buf[...],
            all_taps[:, pl.ds(col0, block)],
            (((1,), (1,)), ((), ())),
            preferred_element_type=jnp.float32,
        )
        return carry

    lax.fori_loop(0, blocks, tap_body, 0)
    own_attn = pltpu.make_async_copy(
        attn_buf.at[rows_of(me), :], attn_ref.at[:, cols_of(me)], local_sem.at[6]
    )
    own_attn.start()
    arrive(3)

    def signal_body(at, carry):
        row0 = pl.multiple_of(at * block, block)
        arrived = all_gate[pl.ds(row0, block), :]
        gated = arrived.astype(jnp.float32) * attn_buf[pl.ds(row0, block), :].astype(jnp.float32)
        ready = (me >= half) & (at < half * per_row)
        gated = jnp.where(ready, arrived, gated.astype(jnp.bfloat16))
        sig_spec[at] = jnp.dot(forward_buf[...], gated, preferred_element_type=jnp.float32)
        return carry

    lax.fori_loop(0, blocks, signal_body, 0)

    lift = 8

    def product_body(at, carry):
        real = pl.ds(pl.multiple_of(at * lift, lift), lift)
        imag = pl.ds(pl.multiple_of(block + at * lift, lift), lift)
        odd = lax.rem(lax.broadcasted_iota(jnp.int32, (lift, width), 0), 2) == 1
        sign = jnp.where(odd, -1.0, 1.0).astype(jnp.float32)
        tap_real = []
        tap_imag = []
        for k in range(blocks):
            now_real = tap_spec[k, real, :]
            now_imag = tap_spec[k, imag, :]
            if k > 0:
                now_real = now_real - sign * tap_spec[k - 1, imag, :]
                now_imag = now_imag + sign * tap_spec[k - 1, real, :]
            tap_real.append(now_real)
            tap_imag.append(now_imag)
        for out in range(blocks):
            sum_real = jnp.zeros((lift, width), jnp.float32)
            sum_imag = jnp.zeros((lift, width), jnp.float32)
            for j in range(out + 1):
                sig_real = sig_spec[j, real, :]
                sig_imag = sig_spec[j, imag, :]
                sum_real = sum_real + sig_real * tap_real[out - j] - sig_imag * tap_imag[out - j]
                sum_imag = sum_imag + sig_real * tap_imag[out - j] + sig_imag * tap_real[out - j]
            prod_spec[out, real, :] = sum_real
            prod_spec[out, imag, :] = sum_imag
        return carry

    lax.fori_loop(0, block // lift, product_body, 0)

    def mixed_send(step):
        peer = lax.rem(me + step, groups)
        sends[6, step] = remote(
            lambda: (mixed_buf.at[rows_of(peer), :], mixed_back.at[:, cols_of(me)]), 6, step
        )
        sends[6, step].start()

    for place, step in enumerate(order):
        group = lax.rem(me + step, groups)

        def inverse_body(at, carry, group=group):
            index = group * per_row + at
            mixed = jnp.dot(
                inverse_buf[...],
                prod_spec[index].astype(jnp.bfloat16),
                preferred_element_type=jnp.float32,
            ).astype(jnp.bfloat16)
            mixed_buf[pl.ds(pl.multiple_of(index * block, block), block), :] = mixed
            return carry

        lax.fori_loop(0, per_row, inverse_body, 0)
        if place > 0:
            mixed_send(order[place - 1])

    own_mixed = pltpu.make_async_copy(
        mixed_buf.at[rows_of(me), :], mixed_back.at[:, cols_of(me)], local_sem.at[5]
    )
    own_mixed.start()
    for step in range(1, groups):
        sends[6, step].wait_recv()
    own_mixed.wait()
    own_attn.wait()
    pl.when(lower)(near_out.wait)
    for step in range(1, groups):
        source = lax.rem(me + groups - step, groups)
        guarded(goes(5, source, me), sends[5, step].wait_recv)
    for (kind, step), copy in sends.items():
        if kind >= 7:
            guarded(me + step < half, copy.wait_send)
        else:
            guarded(goes(kind, me, lax.rem(me + step, groups)), copy.wait_send)


def fused_body(queries, key_rows, values, doc_lengths, in_gate, out_gate, filter_taps):
    rows, channels = queries.shape
    groups = lax.axis_size("ctx")
    width = channels // groups
    length = rows * groups
    block = BLOCK
    blocks = length // block
    forward, inverse = block_tables(block)
    near = groups // 2
    far = (groups - near) * width
    anywhere = pl.BlockSpec(memory_space=pl.ANY)
    half = jnp.bfloat16
    full = jnp.float32
    attended, mixed = pl.pallas_call(
        fused_kernel,
        out_shape=(
            jax.ShapeDtypeStruct((rows, channels), half),
            jax.ShapeDtypeStruct((rows, channels), half),
        ),
        in_specs=[pl.BlockSpec(memory_space=pltpu.SMEM)] + [anywhere] * 7,
        out_specs=(anywhere, anywhere),
        scratch_shapes=[
            pltpu.VMEM((rows, far), half),
            pltpu.VMEM((near * rows, far), half),
            pltpu.VMEM((near * rows, far), half),
            pltpu.VMEM((rows, far), half),
            pltpu.VMEM((rows, far), half),
            pltpu.VMEM((rows, far), half),
            pltpu.VMEM(filter_taps.shape, full),
            pltpu.VMEM(filter_taps.shape, half),
            pltpu.VMEM(forward.shape, half),
            pltpu.VMEM(inverse.shape, half),
            pltpu.VMEM((length, width), half),
            pltpu.VMEM((length, width), half),
            pltpu.VMEM((length, width), half),
            pltpu.VMEM((length, width), half),
            pltpu.VMEM((width, length), half),
            pltpu.VMEM((min(KV_REACH + 1, groups), block, rows), full),
            pltpu.VMEM((length, width), half),
            pltpu.VMEM((blocks, 2 * block, width), full),
            pltpu.VMEM((blocks, 2 * block, width), full),
            pltpu.VMEM((blocks, 2 * block, width), full),
            pltpu.VMEM((length, width), half),
            pltpu.SemaphoreType.DMA((9, groups)),
            pltpu.SemaphoreType.DMA((9, groups)),
            pltpu.SemaphoreType.DMA((7,)),
            pltpu.SemaphoreType.DMA((8,)),
        ],
        compiler_params=pltpu.CompilerParams(
            collective_id=0, has_side_effects=True, vmem_limit_bytes=67043328
        ),
        name="fused_window",
    )(
        doc_lengths,
        queries,
        key_rows,
        values,
        in_gate,
        filter_taps,
        forward,
        inverse,
    )
    hyena_out = (out_gate.astype(full) * mixed.astype(full)).astype(half)
    return (attended, hyena_out)


def fits_fused(queries):
    rows, channels = queries.shape
    groups = lax.axis_size("ctx")
    return channels == groups * HEAD_DIM and rows % BLOCK == 0


def either_body(queries, *rest):
    if fits_fused(queries):
        return fused_body(queries, *rest)
    return body(queries, *rest)


def solution(mesh):
    return jax.shard_map(
        either_body,
        mesh=mesh,
        in_specs=(
            P(("dp", "ctx"), "tp"),
            P(("dp", "ctx"), "tp"),
            P(("dp", "ctx"), "tp"),
            P("dp"),
            P(("dp", "ctx"), "tp"),
            P(("dp", "ctx"), "tp"),
            P(("dp", "tp"), "ctx"),
        ),
        out_specs=(P(("dp", "ctx"), "tp"), P(("dp", "ctx"), "tp")),
        check_vma=False,
    )
```

```python
import functools
import math

import jax
import jax.numpy as jnp
import numpy as np
from jax import lax
from jax.experimental import pallas as pl
from jax.experimental.pallas import tpu as pltpu
from jax.sharding import PartitionSpec as P

HEAD_DIM = 128
KV_REACH = 3
BLOCK = 256


masked_score = -1e30


def passed_along(x, axis, by):
    length = lax.axis_size(axis)
    pairs = [(i, i + by) for i in range(length) if 0 <= i + by < length]
    return lax.ppermute(x, axis, pairs)


def doc_of(positions, doc_lengths):
    starts = jnp.cumsum(doc_lengths) - doc_lengths
    inside = (starts[None, :] <= positions[:, None]).astype(jnp.int32)
    return jnp.sum(inside, axis=1) - 1


def attend_block(carried, pair, query_heads, allowed):
    running_max, running_sum, weighted = carried
    row_count = query_heads.shape[0]
    key_heads = pair[0].reshape(row_count, -1, HEAD_DIM)
    value_heads = pair[1].reshape(row_count, -1, HEAD_DIM)
    scores = jnp.einsum(
        "qhd,khd->hqk", query_heads, key_heads, preferred_element_type=jnp.float32
    ) / math.sqrt(HEAD_DIM)
    scores = jnp.where(allowed[None], scores, masked_score)
    new_max = jnp.maximum(running_max, jnp.max(scores, axis=2))
    rescale = jnp.exp(running_max - new_max)
    exp_scores = jnp.exp(scores - new_max[:, :, None])
    running_sum = running_sum * rescale + jnp.sum(exp_scores, axis=2)
    weighted = weighted * rescale[:, :, None] + jnp.einsum(
        "hqk,khd->hqd",
        exp_scores.astype(jnp.bfloat16),
        value_heads,
        preferred_element_type=jnp.float32,
    )
    return (new_max, running_sum, weighted)


def split_parts(source):
    high_part = lax.optimization_barrier(source.astype(jnp.bfloat16))
    low_part = (source - high_part.astype(jnp.float32)).astype(jnp.bfloat16)
    return (high_part, low_part)


def split_mul(form, left_parts, right_parts):
    first = jnp.einsum(form, left_parts[0], right_parts[0], preferred_element_type=jnp.float32)
    second = jnp.einsum(form, left_parts[0], right_parts[1], preferred_element_type=jnp.float32)
    third = jnp.einsum(form, left_parts[1], right_parts[0], preferred_element_type=jnp.float32)
    return first + (second + third)


def dft_tables(length):
    inner_len = math.gcd(length, 256)
    outer_len = 2 * length // inner_len
    freq_rows = jnp.arange(outer_len, dtype=jnp.int32)
    time_rows = jnp.arange(outer_len // 2, dtype=jnp.int32)
    inner_index = jnp.arange(inner_len, dtype=jnp.int32)
    angle_outer = (
        2.0
        * math.pi
        / outer_len
        * (freq_rows[:, None] * time_rows[None, :] % outer_len).astype(jnp.float32)
    )
    angle_twist = (
        2.0
        * math.pi
        / (2 * length)
        * (freq_rows[:, None] * inner_index[None, :] % (2 * length)).astype(jnp.float32)
    )
    angle_inner = (
        2.0
        * math.pi
        / inner_len
        * (inner_index[:, None] * inner_index[None, :] % inner_len).astype(jnp.float32)
    )
    return (
        split_parts(jnp.cos(angle_outer)),
        split_parts(-jnp.sin(angle_outer)),
        jnp.cos(angle_twist),
        -jnp.sin(angle_twist),
        split_parts(jnp.cos(angle_inner)),
        split_parts(-jnp.sin(angle_inner)),
    )


def right_mul(left_parts, table_parts):
    return split_mul("cin,nm->cim", left_parts, table_parts)


def forward_dft(samples, tables):
    outer_cos, outer_sin, twist_cos, twist_sin, inner_cos, inner_sin = tables
    item_count = samples.shape[0]
    shaped = split_parts(samples.reshape(item_count, outer_cos[0].shape[1], inner_cos[0].shape[0]))
    section_real = split_mul("ij,cjn->cin", outer_cos, shaped)
    section_imag = split_mul("ij,cjn->cin", outer_sin, shaped)
    turned_real = split_parts(section_real * twist_cos - section_imag * twist_sin)
    turned_imag = split_parts(section_real * twist_sin + section_imag * twist_cos)
    spec_real = right_mul(turned_real, inner_cos) - right_mul(turned_imag, inner_sin)
    spec_imag = right_mul(turned_real, inner_sin) + right_mul(turned_imag, inner_cos)
    return (spec_real, spec_imag)


def inverse_dft(prod_real, prod_imag, tables):
    outer_cos, outer_sin, twist_cos, twist_sin, inner_cos, inner_sin = tables
    item_count = prod_real.shape[0]
    half_len = outer_cos[0].shape[1]
    inner_len = inner_cos[0].shape[0]
    real_parts = split_parts(prod_real)
    imag_parts = split_parts(prod_imag)
    back_real = right_mul(real_parts, inner_cos) + right_mul(imag_parts, inner_sin)
    back_imag = right_mul(imag_parts, inner_cos) - right_mul(real_parts, inner_sin)
    unturn_real = split_parts(back_real * twist_cos + back_imag * twist_sin)
    unturn_imag = split_parts(back_imag * twist_cos - back_real * twist_sin)
    rows_out = split_mul("ij,cin->cjn", outer_cos, unturn_real) + split_mul(
        "ij,cin->cjn", outer_sin, unturn_imag
    )
    return (rows_out * (1.0 / (2 * half_len * inner_len))).reshape(item_count, half_len * inner_len)


def filter_apply(signal, filter_spec, tables):
    sig_real, sig_imag = forward_dft(signal, tables)
    tap_real, tap_imag = filter_spec
    prod_real = sig_real * tap_real - sig_imag * tap_imag
    prod_imag = sig_real * tap_imag + sig_imag * tap_real
    return inverse_dft(prod_real, prod_imag, tables)


def body(queries, key_rows, values, doc_lengths, in_gate, out_gate, filter_taps):
    row_count, channels = queries.shape
    head_count = channels // HEAD_DIM
    group_count = lax.axis_size("ctx")
    per_group = channels // group_count
    seq_len = row_count * group_count
    tables = dft_tables(seq_len)
    taps_grouped = filter_taps.reshape(group_count, per_group, row_count)
    query_pos = lax.axis_index("ctx") * row_count + jnp.arange(row_count, dtype=jnp.int32)
    query_doc = doc_of(query_pos, doc_lengths)
    query_heads = queries.reshape(row_count, head_count, HEAD_DIM)
    carried = (
        jnp.full((head_count, row_count), masked_score, jnp.float32),
        jnp.zeros((head_count, row_count), jnp.float32),
        jnp.zeros((head_count, row_count, HEAD_DIM), jnp.float32),
    )

    def visit(state_now, pair, distance):
        key_pos = query_pos - distance * row_count
        key_doc = doc_of(key_pos, doc_lengths)
        allowed = (key_doc[None, :] == query_doc[:, None]) & (
            key_pos[None, :] <= query_pos[:, None]
        )
        return lax.cond(
            jnp.any(allowed),
            lambda state_in: attend_block(state_in, pair, query_heads, allowed),
            lambda state_in: state_in,
            state_now,
        )

    own_pair = jnp.stack((key_rows, values))
    carried = visit(carried, own_pair, 0)
    moving = own_pair
    for distance in range(1, KV_REACH + 1):
        moving = passed_along(moving, "ctx", 1)
        carried = visit(carried, moving, distance)
    running_max, running_sum, weighted = carried
    attended = (
        (weighted / running_sum[:, :, None])
        .transpose(1, 0, 2)
        .reshape(row_count, channels)
        .astype(jnp.bfloat16)
    )
    gated = (in_gate.astype(jnp.float32) * attended.astype(jnp.float32)).T
    gated_grouped = gated.reshape(group_count, per_group, row_count)
    pair = (
        lax.all_to_all(
            gated_grouped.astype(jnp.bfloat16), "ctx", split_axis=0, concat_axis=2, tiled=True
        ).astype(gated_grouped.dtype),
        lax.all_to_all(
            taps_grouped.astype(jnp.bfloat16), "ctx", split_axis=0, concat_axis=2, tiled=True
        ).astype(taps_grouped.dtype),
    )
    item_count = pair[0].shape[1]
    signal = pair[0].reshape(item_count, -1)
    taps = pair[1].reshape(item_count, -1)
    result = filter_apply(signal, forward_dft(taps, tables), tables)
    mixed = result.reshape(1, item_count, -1)
    returned = lax.all_to_all(
        mixed.astype(jnp.bfloat16), "ctx", split_axis=2, concat_axis=0, tiled=True
    ).astype(mixed.dtype)
    hyena_out = (out_gate.astype(jnp.float32) * returned.reshape(channels, row_count).T).astype(
        jnp.bfloat16
    )
    return (attended, hyena_out)


def block_tables(block):
    freq = np.arange(block)
    time = np.arange(block)
    angle = np.pi / (2 * block) * ((2 * freq[:, None] + 1) * time[None, :] % (4 * block))
    forward = np.concatenate((np.cos(angle), -np.sin(angle)), axis=0)
    inverse = forward.T / block
    return (jnp.asarray(forward, jnp.bfloat16), jnp.asarray(inverse, jnp.bfloat16))


def fused_kernel(
    docs_ref,
    query_ref,
    key_ref,
    value_ref,
    gate_ref,
    taps_ref,
    forward_ref,
    inverse_ref,
    attn_ref,
    mixed_back,
    near_query,
    near_key,
    near_value,
    near_gate,
    near_attn,
    near_gated,
    wide_taps,
    half_taps,
    forward_buf,
    inverse_buf,
    all_query,
    all_key,
    all_value,
    all_gate,
    all_taps,
    score_buf,
    attn_buf,
    sig_spec,
    tap_spec,
    prod_spec,
    mixed_buf,
    send_sem,
    recv_sem,
    local_sem,
    table_sem,
):
    rows, _ = query_ref.shape
    length, width = all_query.shape
    groups = length // rows
    block = inverse_ref.shape[0]
    half = groups // 2
    half_cols = pl.ds(half * width, width * (groups - half))
    blocks = length // block
    per_row = rows // block
    me = lax.axis_index("ctx")
    lower = me < half

    def rows_of(group):
        return pl.ds(pl.multiple_of(group * rows, rows), rows)

    def cols_of(group):
        return pl.ds(pl.multiple_of(group * width, width), width)

    barrier = pltpu.get_barrier_semaphore()
    for step in range(1, groups):
        peer = lax.rem(me + step, groups)
        pl.semaphore_signal(
            barrier, inc=1, device_id={"ctx": peer}, device_id_type=pl.DeviceIdType.MESH
        )
    pl.semaphore_wait(barrier, groups - 1)

    class Later:
        def __init__(self, make):
            self.make = make

        def start(self):
            self.make().start()

        def wait(self):
            self.make().wait()

        def wait_recv(self):
            self.make().wait_recv()

        def wait_send(self):
            self.make().wait_send()

    def remote(refs, kind, step):
        def make():
            source, target = refs()
            return pltpu.make_async_remote_copy(
                src_ref=source,
                dst_ref=target,
                send_sem=send_sem.at[kind, step],
                recv_sem=recv_sem.at[kind, step],
                device_id={"ctx": lax.rem(me + step, groups)},
                device_id_type=pl.DeviceIdType.MESH,
            )

        return Later(make)

    def inbound(kind, step):
        peer = lax.rem(me + step, groups)
        source_of = (query_ref, key_ref, value_ref, gate_ref)
        target_of = (all_query, all_key, all_value, all_gate)
        if kind == 4:
            return (
                half_taps.at[cols_of(peer), :],
                all_taps.at[:, rows_of(me)],
            )
        return (source_of[kind].at[:, cols_of(peer)], target_of[kind].at[rows_of(me), :])

    def goes(kind, source, target):
        if kind == 0:
            return (source >= half) | (target < half)
        if kind == 5:
            return (source < half) | (target >= half)
        return None

    def guarded(condition, action):
        if condition is None:
            action()
        else:
            pl.when(condition)(action)

    sends = {}
    own = {}

    def make_send(kind, step):
        sends[kind, step] = remote(lambda: inbound(kind, step), kind, step)

    def near_copy(kind, step):
        source = (key_ref, value_ref)[kind - 7]
        target = (near_key, near_value)[kind - 7]
        return remote(
            lambda: (source.at[:, half_cols], target.at[rows_of(me), :]), kind, step
        )

    def own_copy(refs, place):
        def make():
            source, target = refs()
            return pltpu.make_async_copy(source, target, table_sem.at[place])

        own[place] = Later(make)
        own[place].start()

    for kind in (7, 8):
        for step in range(1, half):
            sends[kind, step] = near_copy(kind, step)
            pl.when(me + step < half)(sends[kind, step].start)
    for kind in range(4):
        for step in range(1, groups):
            make_send(kind, step)
            peer = lax.rem(me + step, groups)
            guarded(
                goes(0, me, peer) if kind in (0, 3) else None, sends[kind, step].start
            )

    @pl.when(lower)
    def _():
        own_copy(lambda: (query_ref.at[:, half_cols], near_query), 0)
        own_copy(lambda: (key_ref.at[:, half_cols], near_key.at[rows_of(me), :]), 1)
        own_copy(lambda: (value_ref.at[:, half_cols], near_value.at[rows_of(me), :]), 2)
        own_copy(lambda: (gate_ref.at[:, half_cols], near_gate), 3)

    own_copy(lambda: (taps_ref, wide_taps), 4)
    own_copy(lambda: (forward_ref, forward_buf), 5)
    own_copy(lambda: (inverse_ref, inverse_buf), 6)
    local = {}
    for kind in range(4):
        source, target = inbound(kind, 0)
        local[kind] = pltpu.make_async_copy(source, target, local_sem.at[kind])
        local[kind].start()

    def arrive(kind):
        local[kind].wait()
        for step in range(1, groups):
            source = lax.rem(me + groups - step, groups)
            guarded(goes(kind, source, me), sends[kind, step].wait_recv)

    starts = []
    total = 0
    for doc in range(docs_ref.shape[0]):
        starts.append(total)
        total = total + docs_ref[doc]

    def query_tile(group, at, query, key_of, value_of):
        first = jnp.maximum(group - KV_REACH, 0)
        row_pos = lax.broadcasted_iota(jnp.int32, (block, width), 0) + (group * rows + at * block)
        row_start = jnp.zeros((block, width), jnp.int32)
        for start in starts:
            row_start = jnp.where(row_pos >= start, start, row_start)
        row_pos = row_pos[:, :1]
        row_start = row_start[:, :1]
        lane_pos = lax.broadcasted_iota(jnp.int32, (block, rows), 1)

        def score_step(chunk, top, last=False):
            scores = lax.dot_general(
                query,
                key_of(rows_of(chunk)),
                (((1,), (1,)), ((), ())),
                preferred_element_type=jnp.float32,
            )
            allowed = lane_pos >= row_start - chunk * rows
            if last:
                allowed = allowed & (lane_pos <= row_pos - chunk * rows)
            scores = jnp.where(allowed, scores, masked_score)
            score_buf[chunk - first] = scores
            for part in range(0, rows, width):
                top = jnp.maximum(top, scores[:, part : part + width])
            return top

        top = jnp.full((block, width), masked_score, jnp.float32)
        top = lax.fori_loop(first, group, score_step, top)
        top = score_step(group, top, last=True)
        top = jnp.max(top, axis=1, keepdims=True)

        def value_step(chunk, carried):
            running, weighted = carried
            weight = jnp.exp2(
                (score_buf[chunk - first] - top) * (math.log2(math.e) / math.sqrt(HEAD_DIM))
            )
            for part in range(0, rows, width):
                running = running + weight[:, part : part + width]
            weighted = weighted + jnp.dot(
                weight.astype(jnp.bfloat16),
                value_of(rows_of(chunk)),
                preferred_element_type=jnp.float32,
            )
            return (running, weighted)

        zero = jnp.zeros((block, width), jnp.float32)
        running, weighted = lax.fori_loop(first, group + 1, value_step, (zero, zero))
        running = jnp.sum(running, axis=1, keepdims=True)
        return (weighted / running).astype(jnp.bfloat16)

    def near_send(head):
        for step in range(1, groups):
            peer = lax.rem(me + step, groups)

            @pl.when(lower & (peer == half + head))
            def _(step=step):
                remote(
                    lambda: (
                        near_gated.at[:, pl.ds(head * width, width)],
                        all_gate.at[rows_of(me), :],
                    ),
                    3,
                    step,
                ).start()

    @pl.when(lower)
    def _():
        for place in range(4):
            own[place].wait()
        for kind in (7, 8):
            for step in range(1, half):
                pl.when(me - step >= 0)(sends[kind, step].wait_recv)
        for head in range(groups - half):
            cols = pl.ds(head * width, width)

            def near_body(at, carry, cols=cols):
                part = pl.ds(pl.multiple_of(at * block, block), block)
                attended = query_tile(
                    me,
                    at,
                    near_query[part, cols],
                    lambda rows_at: near_key[rows_at, cols],
                    lambda rows_at: near_value[rows_at, cols],
                )
                near_attn[part, cols] = attended
                near_gated[part, cols] = (
                    near_gate[part, cols].astype(jnp.float32) * attended.astype(jnp.float32)
                ).astype(jnp.bfloat16)
                return carry

            lax.fori_loop(0, per_row, near_body, 0)
            if head > 0:
                near_send(head - 1)

    own[4].wait()

    def round_body(at, carry):
        part = pl.ds(pl.multiple_of(at * 64, 64), 64)
        half_taps[part, :] = wide_taps[part, :].astype(jnp.bfloat16)
        return carry

    lax.fori_loop(0, half_taps.shape[0] // 64, round_body, 0)
    near_send(groups - half - 1)
    near_out = Later(
        lambda: pltpu.make_async_copy(near_attn, attn_ref.at[:, half_cols], table_sem.at[7])
    )
    pl.when(lower)(near_out.start)

    arrive(0)
    for step in range(1, groups):
        make_send(4, step)
        sends[4, step].start()
    source, target = inbound(4, 0)
    local[4] = pltpu.make_async_copy(source, target, local_sem.at[4])
    local[4].start()
    arrive(1)
    arrive(2)

    def attn_send(step):
        peer = lax.rem(me + step, groups)
        sends[5, step] = remote(
            lambda: (attn_buf.at[rows_of(peer), :], attn_ref.at[:, cols_of(me)]), 5, step
        )
        guarded(goes(5, me, peer), sends[5, step].start)

    order = list(range(1, groups)) + [0]
    for place, step in enumerate(order):
        group = lax.rem(me + step, groups)

        def tile_body(at, carry, group=group):
            tile = group * per_row + at
            part = pl.ds(pl.multiple_of(tile * block, block), block)
            attn_buf[part, :] = query_tile(
                group,
                at,
                all_query[part, :],
                lambda rows_at: all_key[rows_at, :],
                lambda rows_at: all_value[rows_at, :],
            )
            return carry

        @pl.when(goes(5, me, group))
        def _(tile_body=tile_body):
            lax.fori_loop(0, per_row, tile_body, 0)

        if place > 0:
            attn_send(order[place - 1])

    own[5].wait()
    own[6].wait()
    own_attn = pltpu.make_async_copy(
        attn_buf.at[rows_of(me), :], attn_ref.at[:, cols_of(me)], local_sem.at[6]
    )
    own_attn.start()
    arrive(3)

    def signal_body(at, carry):
        row0 = pl.multiple_of(at * block, block)
        arrived = all_gate[pl.ds(row0, block), :]
        gated = arrived.astype(jnp.float32) * attn_buf[pl.ds(row0, block), :].astype(jnp.float32)
        ready = (me >= half) & (at < half * per_row)
        gated = jnp.where(ready, arrived, gated.astype(jnp.bfloat16))
        sig_spec[at] = jnp.dot(forward_buf[...], gated, preferred_element_type=jnp.float32)
        return carry

    lax.fori_loop(0, blocks, signal_body, 0)

    def tap_body(at, carry):
        col0 = pl.multiple_of(at * block, block)
        tap_spec[at] = lax.dot_general(
            forward_buf[...],
            all_taps[:, pl.ds(col0, block)],
            (((1,), (1,)), ((), ())),
            preferred_element_type=jnp.float32,
        )
        return carry

    for step in range(groups):
        if step == 0:
            local[4].wait()
        else:
            sends[4, step].wait_recv()
        group = lax.rem(me + groups - step, groups)
        lax.fori_loop(group * per_row, (group + 1) * per_row, tap_body, 0)

    lift = 8

    def product_body(group, at, carry):
        real = pl.ds(pl.multiple_of(at * lift, lift), lift)
        imag = pl.ds(pl.multiple_of(block + at * lift, lift), lift)
        odd = lax.rem(lax.broadcasted_iota(jnp.int32, (lift, width), 0), 2) == 1
        sign = jnp.where(odd, -1.0, 1.0).astype(jnp.float32)
        tap_real = []
        tap_imag = []
        for k in range((group + 1) * per_row):
            now_real = tap_spec[k, real, :]
            now_imag = tap_spec[k, imag, :]
            if k > 0:
                now_real = now_real - sign * tap_spec[k - 1, imag, :]
                now_imag = now_imag + sign * tap_spec[k - 1, real, :]
            tap_real.append(now_real)
            tap_imag.append(now_imag)
        for out in range(group * per_row, (group + 1) * per_row):
            sum_real = jnp.zeros((lift, width), jnp.float32)
            sum_imag = jnp.zeros((lift, width), jnp.float32)
            for j in range(out + 1):
                sig_real = sig_spec[j, real, :]
                sig_imag = sig_spec[j, imag, :]
                sum_real = sum_real + sig_real * tap_real[out - j] - sig_imag * tap_imag[out - j]
                sum_imag = sum_imag + sig_real * tap_imag[out - j] + sig_imag * tap_real[out - j]
            prod_spec[out, real, :] = sum_real
            prod_spec[out, imag, :] = sum_imag
        return carry

    def inverse_body(at, carry):
        mixed = jnp.dot(
            inverse_buf[...],
            prod_spec[at].astype(jnp.bfloat16),
            preferred_element_type=jnp.float32,
        ).astype(jnp.bfloat16)
        mixed_buf[pl.ds(pl.multiple_of(at * block, block), block), :] = mixed
        return carry

    def mixed_send(group):
        for step in range(1, groups):

            @pl.when(lax.rem(me + step, groups) == group)
            def _(step=step):
                sends[6, step].start()

    for step in range(1, groups):
        sends[6, step] = remote(
            lambda step=step: (
                mixed_buf.at[rows_of(lax.rem(me + step, groups)), :],
                mixed_back.at[:, cols_of(me)],
            ),
            6,
            step,
        )
    for group in range(groups):
        lax.fori_loop(0, block // lift, functools.partial(product_body, group), 0)
        if group > 0:
            mixed_send(group - 1)
        lax.fori_loop(group * per_row, (group + 1) * per_row, inverse_body, 0)
    mixed_send(groups - 1)
    own_mixed = pltpu.make_async_copy(
        mixed_buf.at[rows_of(me), :], mixed_back.at[:, cols_of(me)], local_sem.at[5]
    )
    own_mixed.start()
    for step in range(1, groups):
        sends[6, step].wait_recv()
    own_mixed.wait()
    own_attn.wait()
    pl.when(lower)(near_out.wait)
    for step in range(1, groups):
        source = lax.rem(me + groups - step, groups)
        guarded(goes(5, source, me), sends[5, step].wait_recv)
    for (kind, step), copy in sends.items():
        if kind >= 7:
            guarded(me + step < half, copy.wait_send)
        else:
            guarded(goes(kind, me, lax.rem(me + step, groups)), copy.wait_send)


def fused_body(queries, key_rows, values, doc_lengths, in_gate, out_gate, filter_taps):
    rows, channels = queries.shape
    groups = lax.axis_size("ctx")
    width = channels // groups
    length = rows * groups
    block = BLOCK
    blocks = length // block
    forward, inverse = block_tables(block)
    near = groups // 2
    far = (groups - near) * width
    anywhere = pl.BlockSpec(memory_space=pl.ANY)
    half = jnp.bfloat16
    full = jnp.float32
    attended, mixed = pl.pallas_call(
        fused_kernel,
        out_shape=(
            jax.ShapeDtypeStruct((rows, channels), half),
            jax.ShapeDtypeStruct((rows, channels), half),
        ),
        in_specs=[pl.BlockSpec(memory_space=pltpu.SMEM)] + [anywhere] * 7,
        out_specs=(anywhere, anywhere),
        scratch_shapes=[
            pltpu.VMEM((rows, far), half),
            pltpu.VMEM((near * rows, far), half),
            pltpu.VMEM((near * rows, far), half),
            pltpu.VMEM((rows, far), half),
            pltpu.VMEM((rows, far), half),
            pltpu.VMEM((rows, far), half),
            pltpu.VMEM(filter_taps.shape, full),
            pltpu.VMEM(filter_taps.shape, half),
            pltpu.VMEM(forward.shape, half),
            pltpu.VMEM(inverse.shape, half),
            pltpu.VMEM((length, width), half),
            pltpu.VMEM((length, width), half),
            pltpu.VMEM((length, width), half),
            pltpu.VMEM((length, width), half),
            pltpu.VMEM((width, length), half),
            pltpu.VMEM((min(KV_REACH + 1, groups), block, rows), full),
            pltpu.VMEM((length, width), half),
            pltpu.VMEM((blocks, 2 * block, width), full),
            pltpu.VMEM((blocks, 2 * block, width), full),
            pltpu.VMEM((blocks, 2 * block, width), full),
            pltpu.VMEM((length, width), half),
            pltpu.SemaphoreType.DMA((9, groups)),
            pltpu.SemaphoreType.DMA((9, groups)),
            pltpu.SemaphoreType.DMA((7,)),
            pltpu.SemaphoreType.DMA((8,)),
        ],
        compiler_params=pltpu.CompilerParams(
            collective_id=0, has_side_effects=True, vmem_limit_bytes=67043328
        ),
        name="fused_window",
    )(
        doc_lengths,
        queries,
        key_rows,
        values,
        in_gate,
        filter_taps,
        forward,
        inverse,
    )
    hyena_out = (out_gate.astype(full) * mixed.astype(full)).astype(half)
    return (attended, hyena_out)


def fits_fused(queries):
    rows, channels = queries.shape
    groups = lax.axis_size("ctx")
    return channels == groups * HEAD_DIM and rows % BLOCK == 0


def either_body(queries, *rest):
    if fits_fused(queries):
        return fused_body(queries, *rest)
    return body(queries, *rest)


def solution(mesh):
    return jax.shard_map(
        either_body,
        mesh=mesh,
        in_specs=(
            P(("dp", "ctx"), "tp"),
            P(("dp", "ctx"), "tp"),
            P(("dp", "ctx"), "tp"),
            P("dp"),
            P(("dp", "ctx"), "tp"),
            P(("dp", "ctx"), "tp"),
            P(("dp", "tp"), "ctx"),
        ),
        out_specs=(P(("dp", "ctx"), "tp"), P(("dp", "ctx"), "tp")),
        check_vma=False,
    )
```
